128 devices in a mesh: section: 4 (over z), dp: 32 (over x, y, core).
Axes of the slice: x: 4, y: 4, z: 4, core: 2. Of those that a mesh axis runs over, the one named last changes fastest.
Arguments:
- gradient: float32 [4, 32, 256, 4096], P('section', 'dp'), may hold values from -6 to 6
- dither: int32 [4, 32, 256, 4096], P('section', 'dp'), may hold values from 0 to 255
- sign_bits: int32 [4096], replicated, may hold values from 0 to 1
- levels: float32 [16], replicated, may hold values from -1 to 1, as said below
- layout: int32 [256], replicated, may hold values from 0 to 255, each once
- master: float32 [4, 256, 4096], P('section', 'dp'), may hold values from -6 to 6
- first_moment: float32 [4, 256, 4096], P('section', 'dp'), may hold values from -4 to 4
- second_moment: float32 [4, 256, 4096], P('section', 'dp'), may hold values from 0.05 to 2
Outputs:
- updated_master: float32 [4, 256, 4096], P('section', 'dp')
- updated_first: float32 [4, 256, 4096], P('section', 'dp')
- updated_second: float32 [4, 256, 4096], P('section', 'dp')
- parameters: bfloat16 [4, 256, 4096], P('section')
The draws below stay inside these ranges and needn't reach their ends.
Inputs may be any that keep to these rules, and one draw needn't show every extreme that they name: `levels`: strictly increasing; the first is -1 and the last 1; neighbouring levels differ by at least 1/30. `layout`: each block number once.
All inputs are finite; a program needn't handle non-finite values.
Results may differ from the reference program's by a relative error of at most 0.001.
The reference program's roundings to bfloat16 on the way (of `symbols`) count: a program that leaves them out, or rounds other values in their place, can miss the bound.
Values may be sent and summed in bfloat16 or wider, within the bound.
No kernel may reach another device: no remote copies, remote signals or barrier semaphores. Data moves between devices by JAX's collectives and lax.ppermute only.
A program may use at most 64 MiB of HBM per device.

```python
import math
import jax
import jax.numpy as jnp
from jax import lax

LEVELS = 16
BLOCK = 4096
BLOCKS = 256
N_SECTION = 4
N_DP = 32


def draw_levels(key, part):
    spacing = jax.random.uniform(key, (LEVELS - 1,), jnp.float32, 1.0, 4.0)
    rising = jnp.concatenate([jnp.zeros((1,), jnp.float32), jnp.cumsum(spacing)])
    return -1.0 + 2.0 * rising / rising[-1]


def plant(values, stream_key, least, high):
    dims = values.shape
    spot = [jax.random.randint(jax.random.fold_in(stream_key, axis), (), 0, dims[axis]) for axis in range(len(dims))]
    values = values.at[tuple(spot)].set(least)
    longest = dims.index(max(dims))
    spot[longest] = (spot[longest] + 1) % dims[longest]
    return values.at[tuple(spot)].set(high)


def steps_of(key, extent, pieces, low, top_value):
    gain, own = 1.0, jax.random.fold_in(key, 6)
    for axis_at, shards_of in pieces:
        heights = jnp.exp(jax.random.uniform(jax.random.fold_in(own, axis_at), (shards_of,), jnp.float32, low / len(pieces), top_value / len(pieces)))
        gain = gain * jnp.repeat(heights, extent[axis_at] // shards_of).reshape([-1 if axis == axis_at else 1 for axis in range(len(extent))])
    return gain


def bell_draw(stream_key, dims, width, most, shards=(), held_as=jnp.bfloat16):
    array = width * jax.random.normal(stream_key, dims, jnp.float32)
    if shards:
        array = array * steps_of(stream_key, dims, shards, -0.22, 0.18)
    return jnp.clip(array, -most, most).astype(held_as)


def setup_inputs(seed: int = 0) -> dict:
    splits = jax.random.split(jax.random.key(seed), 9)
    return {
        "gradient": bell_draw(splits[0], (N_SECTION, N_DP, BLOCKS, BLOCK), 1.0, 6.0, ((0, 4), (1, 32)), jnp.float32),
        "dither": plant(jax.random.randint(splits[1], (N_SECTION, N_DP, BLOCKS, BLOCK), 0, 256), jax.random.fold_in(splits[1], 1), 0, 255).astype(jnp.int32),
        "sign_bits": plant(jax.random.randint(splits[2], (BLOCK,), 0, 2), jax.random.fold_in(splits[2], 1), 0, 1).astype(jnp.int32),
        "levels": draw_levels(jax.random.fold_in(splits[8], 71), 0),
        "layout": jax.random.permutation(splits[4], BLOCKS).astype(jnp.int32),
        "master": bell_draw(splits[5], (N_SECTION, BLOCKS, BLOCK), 1.0, 6.0, ((0, 4), (1, 32)), jnp.float32),
        "first_moment": bell_draw(splits[6], (N_SECTION, BLOCKS, BLOCK), 0.5, 4.0, ((0, 4), (1, 32)), jnp.float32),
        "second_moment": jnp.clip(jnp.exp(math.log(2.0) - 3.6888794 * jax.random.uniform(splits[7], (N_SECTION, BLOCKS, BLOCK), jnp.float32) ** steps_of(splits[7], (N_SECTION, BLOCKS, BLOCK), ((0, 4), (1, 32)), -0.2, 0.2)), 0.05, 2.0),
    }


adam_epsilon = 1e-08
learning_rate = 0.02
weight_decay = 0.1
first_decay = 0.9
second_decay = 0.95
dither_steps = 256.0

def hadamard_table(edge_length):
    row_numbers = lax.broadcasted_iota(jnp.int32, (edge_length, edge_length), 0)
    column_numbers = lax.broadcasted_iota(jnp.int32, (edge_length, edge_length), 1)
    common = jnp.bitwise_and(row_numbers, column_numbers)
    parity = jnp.zeros((edge_length, edge_length), jnp.int32)
    for bit_number in range(edge_length.bit_length() - 1):
        parity = parity + jnp.bitwise_and(jnp.right_shift(common, bit_number), 1)
    parity = parity % 2
    return (1 - 2 * parity).astype(jnp.float32)

def square_transform(blocks):
    edge_length = math.isqrt(blocks.shape[-1])
    table = hadamard_table(edge_length)
    folded = blocks.reshape(-1, edge_length, edge_length)
    turned = jnp.einsum('ac,ncd,db->nab', table, folded, table, precision=lax.Precision.HIGHEST)
    return turned.reshape(blocks.shape) / edge_length

def rotate(blocks, flips):
    return square_transform(blocks * flips)

def unrotate(blocks, flips):
    return square_transform(blocks) * flips

def encode(ratios, levels):
    relaxed = jnp.zeros_like(ratios)
    for position in range(levels.shape[0] - 1):
        spacing = levels[position + 1] - levels[position]
        relaxed = relaxed + jnp.clip((ratios - levels[position]) / spacing, 0.0, 1.0)
    return relaxed

def decode(symbols, levels):
    values = jnp.zeros_like(symbols) + levels[0]
    for position in range(levels.shape[0] - 1):
        spacing = levels[position + 1] - levels[position]
        values = values + spacing * jnp.clip(symbols - position, 0.0, 1.0)
    return values

def reference(gradient, dither, sign_bits, levels, layout, master, first_moment, second_moment):
    flips = (1 - 2 * sign_bits).astype(jnp.float32)
    stacked = gradient.reshape(N_SECTION * N_DP, BLOCKS, BLOCK)
    peaks = lax.map(lambda single: lax.optimization_barrier(jnp.max(jnp.abs(rotate(single, flips)), axis=1)), stacked)
    block_scale = lax.optimization_barrier(jnp.max(peaks.reshape(N_SECTION, N_DP, BLOCKS), axis=1)) + 1e-06
    inverse = jnp.argsort(layout).astype(jnp.int32)
    section_grads = []
    for section_number in range(N_SECTION):
        scale_here = block_scale[section_number]

        def accumulate(carry, inputs):
            single, noise = inputs
            ratios = rotate(single, flips) / scale_here[:, None]
            offsets = (noise.astype(jnp.float32) + 0.5) / dither_steps - 0.5
            symbols = (encode(ratios, levels) + offsets).astype(jnp.bfloat16)
            return (carry + decode(symbols.astype(jnp.float32), levels), None)
        summed_codes, _ = lax.scan(accumulate, jnp.zeros((BLOCKS, BLOCK), jnp.float32), (gradient[section_number], dither[section_number]))
        slot_sums = jnp.take(summed_codes, layout, axis=0) * jnp.take(scale_here, layout)[:, None]
        section_grads.append(unrotate(slot_sums, flips))
    grads = jnp.stack(section_grads)
    updated_first = first_decay * first_moment + (1.0 - first_decay) * grads
    updated_second = second_decay * second_moment + (1.0 - second_decay) * grads * grads
    updated_master = master - learning_rate * (updated_first / (jnp.sqrt(updated_second) + adam_epsilon) + weight_decay * master)
    parameters = jnp.take(updated_master.astype(jnp.bfloat16), inverse, axis=1)
    return (updated_master, updated_first, updated_second, parameters)
```

```python
import functools

import jax
import jax.numpy as jnp
from jax import lax
from jax.experimental import pallas as pl
from jax.experimental.pallas import tpu as pltpu
from jax.sharding import Mesh, PartitionSpec as P

adam_epsilon = 1e-08
learning_rate = 0.02
weight_decay = 0.1
first_decay = 0.9
second_decay = 0.95
dither_steps = 256.0

LANES = 128
WIDE = 256
CELLS = 64
CELL_RATE = 31.95
VMEM_BYTES = 48 * 1024 * 1024
OTHER_CORE = ((0, 1), (1, 0))


def hadamard(edge):
    common = lax.broadcasted_iota(jnp.int32, (edge, edge), 0) & lax.broadcasted_iota(jnp.int32, (edge, edge), 1)
    parity = jnp.zeros((edge, edge), jnp.int32)
    for bit in range(edge.bit_length() - 1):
        parity = parity ^ ((common >> bit) & 1)
    return (1 - 2 * parity).astype(jnp.float32)


def three_pieces(values):
    high = values.astype(jnp.bfloat16)
    rest = values - high.astype(jnp.float32)
    middle = rest.astype(jnp.bfloat16)
    low = (rest - middle.astype(jnp.float32)).astype(jnp.bfloat16)
    return high, middle, low


def butterflies(parts):
    parts = list(parts)
    stride = 1
    while stride < len(parts):
        for first in range(len(parts)):
            if not first & stride:
                one, two = parts[first], parts[first + stride]
                parts[first], parts[first + stride] = one + two, one - two
        stride *= 2
    return parts


def times_table(values, table):
    pieces = jnp.concatenate(three_pieces(values), axis=1)
    return jnp.dot(pieces, table, preferred_element_type=jnp.float32)


def looked_up(table, index):
    return jnp.take_along_axis(table, index, axis=1)


def rotate_kernel(gradient_ref, bits_ref, rotated_ref, peaks_ref, table_ref, rows_ref):
    step = pl.program_id(0)
    rows, block = gradient_ref.shape

    @pl.when(step == 0)
    def _():
        table = (hadamard(WIDE) * (1.0 / 64.0)).astype(jnp.bfloat16)
        for piece in range(3):
            table_ref[pl.ds(piece * WIDE, WIDE), :] = table

    flips = (1 - 2 * bits_ref[...]).astype(jnp.float32)
    parts = butterflies(
        gradient_ref[:, at : at + WIDE] * flips[:, at : at + WIDE] for at in range(0, block, WIDE)
    )
    most = jnp.zeros((rows, WIDE), jnp.float32)
    for number, part in enumerate(parts):
        turned = times_table(part, table_ref[...])
        rotated_ref[:, number * WIDE : (number + 1) * WIDE] = turned
        most = jnp.maximum(most, jnp.abs(turned))
    rows_ref[pl.ds(pl.multiple_of(step * rows, rows), rows), :] = jnp.maximum(most[:, :LANES], most[:, LANES:])

    @pl.when(step == pl.num_programs(0) - 1)
    def _():
        blocks = rows_ref.shape[0]
        lines = [
            jnp.max(jnp.transpose(rows_ref[at : at + LANES, :]), axis=0, keepdims=True) for at in range(0, blocks, LANES)
        ]
        lines = jnp.concatenate(lines * (8 // len(lines)), axis=0)
        peaks_ref[...] = jnp.broadcast_to(lines[None], peaks_ref.shape)


def rotate(gradient, bits, groups):
    blocks, block = gradient.shape
    rows = 32
    return pl.pallas_call(
        rotate_kernel,
        grid=(blocks // rows,),
        in_specs=[
            pl.BlockSpec((rows, block), lambda i: (i, 0)),
            pl.BlockSpec((1, block), lambda i: (0, 0)),
        ],
        out_specs=[
            pl.BlockSpec((rows, block), lambda i: (i, 0)),
            pl.BlockSpec((groups, 8, LANES), lambda i: (0, 0, 0)),
        ],
        out_shape=[
            jax.ShapeDtypeStruct((blocks, block), jnp.float32),
            jax.ShapeDtypeStruct((groups, 8, LANES), jnp.float32),
        ],
        scratch_shapes=[pltpu.VMEM((3 * WIDE, WIDE), jnp.bfloat16), pltpu.VMEM((blocks, LANES), jnp.float32)],
        compiler_params=pltpu.CompilerParams(vmem_limit_bytes=VMEM_BYTES),
        name="rotate",
    )(gradient, bits)


def encode_tables(levels_ref):
    count = levels_ref.shape[0]
    lane = lax.broadcasted_iota(jnp.int32, (8, LANES), 1)
    cell = lane & (CELLS - 1)
    threshold = jnp.full((8, LANES), 4.0, jnp.float32)
    position = jnp.zeros((8, LANES), jnp.int32)
    for number in range(1, count - 1):
        level = jnp.full((8, LANES), levels_ref[number], jnp.float32)
        its_cell = (level * CELL_RATE + 32.0).astype(jnp.int32)
        threshold = jnp.where(its_cell == cell, level, threshold)
        before = (its_cell < cell) | ((its_cell == cell) & (lane >= CELLS))
        position = position + before.astype(jnp.int32)
    slope = jnp.zeros((8, LANES), jnp.float32)
    intercept = jnp.zeros((8, LANES), jnp.float32)
    for number in range(count - 1):
        low = jnp.full((8, LANES), levels_ref[number], jnp.float32)
        high = jnp.full((8, LANES), levels_ref[number + 1], jnp.float32)
        its_slope = 1.0 / (high - low)
        its_intercept = (number + (0.5 / dither_steps - 0.5)) - low * its_slope
        slope = jnp.where(position == number, its_slope, slope)
        intercept = jnp.where(position == number, its_intercept, intercept)
    return threshold, slope, intercept


def decode_tables(levels_ref):
    count = levels_ref.shape[0]
    lane = lax.broadcasted_iota(jnp.int32, (8, LANES), 1)
    slope = jnp.zeros((8, LANES), jnp.float32)
    intercept = jnp.full((8, LANES), levels_ref[count - 1], jnp.float32)
    for number in range(count - 1):
        low = jnp.full((8, LANES), levels_ref[number], jnp.float32)
        high = jnp.full((8, LANES), levels_ref[number + 1], jnp.float32)
        slope = jnp.where(lane == number, high - low, slope)
        intercept = jnp.where(lane == number, low - number * (high - low), intercept)
    return slope, intercept


def encode_kernel(levels_ref, rotated_ref, dither_ref, peaks_ref, layout_ref, symbols_ref, scales_ref, inverse_ref, order_ref, held_ref):
    step = pl.program_id(0)
    blocks, columns = rotated_ref.shape

    @pl.when(step == 0)
    def _():
        lines = jnp.max(peaks_ref[...], axis=0) + 1e-06
        wide = jnp.concatenate([lines[i : i + 1, :] for i in range(blocks // LANES)], axis=1)
        order = lax.broadcasted_iota(jnp.int32, (blocks, blocks), 0) == layout_ref[...]
        order = jnp.transpose(order.astype(jnp.float32))
        order_ref[...] = order.astype(jnp.bfloat16)
        slot = jnp.sum(jnp.where(order > 0.5, wide, 0.0), axis=1, keepdims=True)
        scales_ref[...] = jnp.broadcast_to(slot, (blocks, LANES))
        for at in range(blocks // LANES):
            square = jnp.broadcast_to(lines[at : at + 1, :], (LANES, LANES))
            inverse_ref[at * LANES : (at + 1) * LANES, :] = 1.0 / jnp.transpose(square)

    threshold, slope, intercept = encode_tables(levels_ref)

    def eight_rows(number, carry):
        at = pl.multiple_of(number * 16, 16)
        for part in range(columns // LANES):
            pair = []
            for half in range(2):
                here = pl.ds(pl.multiple_of(at + half * 8, 8), 8)
                over = slice(part * LANES, (part + 1) * LANES)
                ratio = rotated_ref[here, over] * inverse_ref[here, :]
                cell = (ratio * CELL_RATE + 32.0).astype(jnp.int32)
                side = jnp.where(ratio >= looked_up(threshold, cell), cell + CELLS, cell)
                value = ratio * looked_up(slope, side) + looked_up(intercept, side)
                pair.append(value + dither_ref[here, over].astype(jnp.float32) * (1.0 / dither_steps))
            held_ref[pl.ds(at, 16), part * LANES : (part + 1) * LANES] = jnp.concatenate(pair, axis=0).astype(jnp.bfloat16)
        return carry

    lax.fori_loop(0, blocks // 16, eight_rows, 0)
    slotted = jnp.dot(order_ref[...], held_ref[...], preferred_element_type=jnp.float32)
    symbols_ref[...] = slotted.astype(jnp.bfloat16)


def encode(rotated, dither, peaks, layout, levels):
    blocks, block = rotated.shape
    columns = 512
    return pl.pallas_call(
        encode_kernel,
        grid=(block // columns,),
        in_specs=[
            pl.BlockSpec(memory_space=pltpu.SMEM),
            pl.BlockSpec((blocks, columns), lambda i: (0, i)),
            pl.BlockSpec((blocks, columns), lambda i: (0, i)),
            pl.BlockSpec(peaks.shape, lambda i: (0, 0, 0)),
            pl.BlockSpec((1, blocks), lambda i: (0, 0)),
        ],
        out_specs=[
            pl.BlockSpec((blocks, columns), lambda i: (0, i)),
            pl.BlockSpec((blocks, LANES), lambda i: (0, 0)),
        ],
        out_shape=[
            jax.ShapeDtypeStruct((blocks, block), jnp.bfloat16),
            jax.ShapeDtypeStruct((blocks, LANES), jnp.float32),
        ],
        scratch_shapes=[
            pltpu.VMEM((blocks, LANES), jnp.float32),
            pltpu.VMEM((blocks, blocks), jnp.bfloat16),
            pltpu.VMEM((blocks, columns), jnp.bfloat16),
        ],
        compiler_params=pltpu.CompilerParams(vmem_limit_bytes=VMEM_BYTES),
        name="encode",
    )(levels, rotated, dither, peaks, layout)


def owner_kernel(
    first_ref, levels_ref, symbols_ref, scales_ref, bits_ref, master_ref, moment_ref, second_ref,
    new_master_ref, new_moment_ref, new_second_ref, copies_ref, total_ref, table_ref,
):
    step = pl.program_id(0)
    rows, block = total_ref.shape
    count = levels_ref.shape[0]
    slope, intercept = decode_tables(levels_ref)

    @pl.when(step == 0)
    def _():
        total_ref[...] = jnp.zeros_like(total_ref)
        table = (hadamard(WIDE) * (1.0 / 64.0)).astype(jnp.bfloat16)
        for piece in range(3):
            table_ref[pl.ds(piece * WIDE, WIDE), :] = table

    def column(number, carry):
        over = pl.ds(pl.multiple_of(number * LANES, LANES), LANES)
        total = total_ref[:, over]
        for replica in range(symbols_ref.shape[0]):
            symbol = symbols_ref[replica, :, over].astype(jnp.float32)
            symbol = jnp.minimum(jnp.maximum(symbol, 0.0), count - 1.0)
            number_of = symbol.astype(jnp.int32)
            total = total + (symbol * looked_up(slope, number_of) + looked_up(intercept, number_of))
        total_ref[:, over] = total
        return carry

    lax.fori_loop(0, block // LANES, column, 0)

    @pl.when(step == pl.num_programs(0) - 1)
    def _():
        flips = (1 - 2 * bits_ref[...]).astype(jnp.float32)
        scales = jnp.concatenate([scales_ref[...]] * (WIDE // LANES), axis=1)
        parts = butterflies(total_ref[:, at : at + WIDE] * scales for at in range(0, block, WIDE))
        for number, part in enumerate(parts):
            over = slice(number * WIDE, (number + 1) * WIDE)
            grads = times_table(part, table_ref[...]) * flips[:, over]
            moment = first_decay * moment_ref[:, over] + (1.0 - first_decay) * grads
            second = second_decay * second_ref[:, over] + (1.0 - second_decay) * grads * grads
            master = master_ref[:, over]
            updated = master - learning_rate * (moment / (jnp.sqrt(second) + adam_epsilon) + weight_decay * master)
            new_moment_ref[:, over] = moment
            new_second_ref[:, over] = second
            new_master_ref[:, over] = updated
            rounded = updated.astype(jnp.bfloat16)
            for copy in range(copies_ref.shape[0]):
                copies_ref[copy, :, over] = rounded


def owner(place, levels, received, scales, bits, master, moment, second, copies):
    replicas, rows, block = received.shape
    each = 8
    whole = pl.BlockSpec((rows, block), lambda i, place: (0, 0))
    return pl.pallas_call(
        owner_kernel,
        grid_spec=pltpu.PrefetchScalarGridSpec(
            num_scalar_prefetch=1,
            grid=(replicas // each,),
            in_specs=[
                pl.BlockSpec(memory_space=pltpu.SMEM),
                pl.BlockSpec((each, rows, block), lambda i, place: (i, 0, 0)),
                pl.BlockSpec((rows, LANES), lambda i, place: (place[0], 0)),
                pl.BlockSpec((1, block), lambda i, place: (0, 0)),
                whole,
                whole,
                whole,
            ],
            out_specs=[whole, whole, whole, pl.BlockSpec((copies, rows, block), lambda i, place: (0, 0, 0))],
            scratch_shapes=[pltpu.VMEM((rows, block), jnp.float32), pltpu.VMEM((3 * WIDE, WIDE), jnp.bfloat16)],
        ),
        out_shape=[jax.ShapeDtypeStruct((rows, block), jnp.float32)] * 3
        + [jax.ShapeDtypeStruct((copies, rows, block), jnp.bfloat16)],
        compiler_params=pltpu.CompilerParams(vmem_limit_bytes=VMEM_BYTES),
        name="owner",
    )(place, levels, received, scales, bits, master, moment, second)


def reorder_kernel(mine_ref, others_ref, my_slots_ref, other_slots_ref, out_ref):
    blocks = out_ref.shape[0]
    half = mine_ref.shape[0]
    row = lax.broadcasted_iota(jnp.int32, (blocks, half), 0)
    my_order = (row == my_slots_ref[...]).astype(jnp.float32).astype(jnp.bfloat16)
    other_order = (row == other_slots_ref[...]).astype(jnp.float32).astype(jnp.bfloat16)
    order = jnp.concatenate([my_order, other_order], axis=1)
    held = jnp.concatenate([mine_ref[...], others_ref[...]], axis=0)
    out_ref[...] = jnp.dot(order, held, preferred_element_type=jnp.float32).astype(jnp.bfloat16)


def reorder(mine, others, my_slots, other_slots):
    half, block = mine.shape
    columns = 1024
    return pl.pallas_call(
        reorder_kernel,
        grid=(block // columns,),
        in_specs=[
            pl.BlockSpec((half, columns), lambda i: (0, i)),
            pl.BlockSpec((half, columns), lambda i: (0, i)),
            pl.BlockSpec((1, half), lambda i: (0, 0)),
            pl.BlockSpec((1, half), lambda i: (0, 0)),
        ],
        out_specs=pl.BlockSpec((2 * half, columns), lambda i: (0, i)),
        out_shape=jax.ShapeDtypeStruct((2 * half, block), jnp.bfloat16),
        compiler_params=pltpu.CompilerParams(vmem_limit_bytes=VMEM_BYTES),
        name="reorder",
    )(mine, others, my_slots, other_slots)


def local(axes, gradient, dither, sign_bits, levels, layout, master, first_moment, second_moment):
    groups = lax.axis_size(axes)
    chips, core = axes[:-1], axes[-1]
    blocks, block = gradient.shape[2:]
    owned = blocks // groups
    bits = sign_bits.reshape(1, block)
    rotated, peaks = rotate(gradient[0, 0], bits, groups)
    peaks = lax.all_to_all(peaks, axes, 0, 0, tiled=True)
    symbols, scales = encode(rotated, dither[0, 0], peaks, layout.reshape(1, blocks), levels)
    received = lax.all_to_all(symbols.reshape(groups, owned, block), axes, 0, 0, tiled=True)
    place = lax.axis_index(axes).reshape(1)
    new_master, new_moment, new_second, copies = owner(
        place, levels, received, scales, bits, master[0], first_moment[0], second_moment[0], groups // 2
    )
    mine = lax.all_to_all(copies, chips, 0, 0, tiled=True)
    others = lax.ppermute(mine, core, OTHER_CORE)
    by_core = layout.reshape(groups // 2, 2, owned)
    which = lax.axis_index(core)
    my_slots = lax.dynamic_index_in_dim(by_core, which, 1, False).reshape(1, blocks // 2)
    other_slots = lax.dynamic_index_in_dim(by_core, 1 - which, 1, False).reshape(1, blocks // 2)
    parameters = reorder(
        mine.reshape(blocks // 2, block), others.reshape(blocks // 2, block), my_slots, other_slots
    )
    return (new_master[None], new_moment[None], new_second[None], parameters[None])


def solution(mesh):
    section, dp = mesh.axis_names
    axes = ("dp_chip", "dp_core")
    split = Mesh(mesh.devices.reshape(mesh.shape[section], mesh.shape[dp] // 2, 2), (section, *axes))
    placed = (
        P(section, axes, None, None),
        P(section, axes, None, None),
        P(),
        P(),
        P(),
        P(section, axes, None),
        P(section, axes, None),
        P(section, axes, None),
    )
    return jax.shard_map(
        functools.partial(local, axes),
        mesh=split,
        in_specs=placed,
        out_specs=(P(section, axes, None), P(section, axes, None), P(section, axes, None), P(section, None, None)),
        check_vma=False,
    )
```

```python
import functools

import jax
import jax.numpy as jnp
from jax import lax
from jax.experimental import pallas as pl
from jax.experimental.pallas import tpu as pltpu
from jax.sharding import Mesh, PartitionSpec as P

adam_epsilon = 1e-08
learning_rate = 0.02
weight_decay = 0.1
first_decay = 0.9
second_decay = 0.95
dither_steps = 256.0

LANES = 128
WIDE = 256
CELLS = 64
CELL_RATE = 31.95
MIB = 1024 * 1024
VMEM_BYTES = 16 * MIB
OTHER_CORE = ((0, 1), (1, 0))


def hadamard(edge):
    common = lax.broadcasted_iota(jnp.int32, (edge, edge), 0) & lax.broadcasted_iota(jnp.int32, (edge, edge), 1)
    parity = jnp.zeros((edge, edge), jnp.int32)
    for bit in range(edge.bit_length() - 1):
        parity = parity ^ ((common >> bit) & 1)
    return (1 - 2 * parity).astype(jnp.float32)


def three_pieces(values):
    high = values.astype(jnp.bfloat16)
    rest = values - high.astype(jnp.float32)
    middle = rest.astype(jnp.bfloat16)
    low = (rest - middle.astype(jnp.float32)).astype(jnp.bfloat16)
    return high, middle, low


def butterflies(parts):
    parts = list(parts)
    stride = 1
    while stride < len(parts):
        for first in range(len(parts)):
            if not first & stride:
                one, two = parts[first], parts[first + stride]
                parts[first], parts[first + stride] = one + two, one - two
        stride *= 2
    return parts


def times_table(values, table):
    pieces = jnp.concatenate(three_pieces(values), axis=1)
    return jnp.dot(pieces, table, preferred_element_type=jnp.float32)


BY_LANE = lax.GatherDimensionNumbers(
    offset_dims=(),
    collapsed_slice_dims=(1,),
    start_index_map=(1,),
    operand_batching_dims=(0,),
    start_indices_batching_dims=(0,),
)


def looked_up(table, index):
    return lax.gather(table, index[..., None], BY_LANE, (1, 1), mode=lax.GatherScatterMode.PROMISE_IN_BOUNDS)


def rotate_kernel(gradient_ref, bits_ref, rotated_ref, peaks_ref, table_ref, rows_ref):
    step = pl.program_id(0)
    rows, block = gradient_ref.shape

    @pl.when(step == 0)
    def _():
        table = (hadamard(WIDE) * (1.0 / 64.0)).astype(jnp.bfloat16)
        for piece in range(3):
            table_ref[pl.ds(piece * WIDE, WIDE), :] = table

    flips = (1 - 2 * bits_ref[...]).astype(jnp.float32)
    parts = butterflies(gradient_ref[:, at : at + WIDE] * flips[:, at : at + WIDE] for at in range(0, block, WIDE))
    turned = times_table(jnp.concatenate(parts, axis=0), table_ref[...])
    most = jnp.zeros((rows, WIDE), jnp.float32)
    for number in range(block // WIDE):
        part = turned[number * rows : (number + 1) * rows]
        rotated_ref[:, number * WIDE : (number + 1) * WIDE] = part
        most = jnp.maximum(most, jnp.abs(part))
    rows_ref[pl.ds(pl.multiple_of(step * rows, rows), rows), :] = jnp.maximum(most[:, :LANES], most[:, LANES:])

    @pl.when(step == pl.num_programs(0) - 1)
    def _():
        blocks = rows_ref.shape[0]
        lines = [
            jnp.max(jnp.transpose(rows_ref[at : at + LANES, :]), axis=0, keepdims=True) for at in range(0, blocks, LANES)
        ]
        lines = jnp.concatenate(lines * (8 // len(lines)), axis=0)
        peaks_ref[...] = jnp.broadcast_to(lines[None], peaks_ref.shape)


def rotate(gradient, bits, groups):
    blocks, block = gradient.shape
    rows = 64
    return pl.pallas_call(
        rotate_kernel,
        grid=(blocks // rows,),
        in_specs=[
            pl.BlockSpec((rows, block), lambda i: (i, 0)),
            pl.BlockSpec((1, block), lambda i: (0, 0)),
        ],
        out_specs=[
            pl.BlockSpec((rows, block), lambda i: (i, 0)),
            pl.BlockSpec((groups, 8, LANES), lambda i: (0, 0, 0)),
        ],
        out_shape=[
            jax.ShapeDtypeStruct((blocks, block), jnp.float32),
            jax.ShapeDtypeStruct((groups, 8, LANES), jnp.float32),
        ],
        scratch_shapes=[pltpu.VMEM((3 * WIDE, WIDE), jnp.bfloat16), pltpu.VMEM((blocks, LANES), jnp.float32)],
        compiler_params=pltpu.CompilerParams(vmem_limit_bytes=49 * MIB),
        name="rotate",
    )(gradient, bits)


def encode_tables(levels_ref):
    count = levels_ref.shape[0]
    lane = lax.broadcasted_iota(jnp.int32, (8, LANES), 1)
    cell = lane & (CELLS - 1)
    threshold = jnp.full((8, LANES), 4.0, jnp.float32)
    position = jnp.zeros((8, LANES), jnp.int32)
    for number in range(1, count - 1):
        level = jnp.full((8, LANES), levels_ref[number], jnp.float32)
        its_cell = (level * CELL_RATE + 32.0).astype(jnp.int32)
        threshold = jnp.where(its_cell == cell, level, threshold)
        before = (its_cell < cell) | ((its_cell == cell) & (lane >= CELLS))
        position = position + before.astype(jnp.int32)
    slope = jnp.zeros((8, LANES), jnp.float32)
    intercept = jnp.zeros((8, LANES), jnp.float32)
    for number in range(count - 1):
        low = jnp.full((8, LANES), levels_ref[number], jnp.float32)
        high = jnp.full((8, LANES), levels_ref[number + 1], jnp.float32)
        its_slope = 1.0 / (high - low)
        its_intercept = (number + (0.5 / dither_steps - 0.5)) - low * its_slope
        slope = jnp.where(position == number, its_slope, slope)
        intercept = jnp.where(position == number, its_intercept, intercept)
    return threshold, slope, intercept


def line_tables(levels_ref):
    lines = []
    for number in range(levels_ref.shape[0] - 1):
        low = jnp.full((8, LANES), levels_ref[number], jnp.float32)
        slope = 1.0 / (jnp.full((8, LANES), levels_ref[number + 1], jnp.float32) - low)
        lines.append((slope, (number + (0.5 / dither_steps - 0.5)) - low * slope))
    return lines


def encode_kernel(
    levels_ref, rotated_ref, dither_ref, peaks_ref, layout_ref, symbols_ref, scales_ref,
    inverse_ref, order_ref, held_ref, tables_ref, lines_ref, out_ref, out_sems,
):
    step = pl.program_id(0)
    blocks, columns = rotated_ref.shape
    count = levels_ref.shape[0]

    @pl.when(step == 0)
    def _():
        lines = jnp.max(peaks_ref[...], axis=0) + 1e-06
        wide = jnp.concatenate([lines[i : i + 1, :] for i in range(blocks // LANES)], axis=1)
        order = lax.broadcasted_iota(jnp.int32, (blocks, blocks), 0) == layout_ref[...]
        order = jnp.transpose(order.astype(jnp.float32))
        order_ref[...] = order.astype(jnp.bfloat16)
        slot = jnp.sum(jnp.where(order > 0.5, wide, 0.0), axis=1, keepdims=True)
        scales_ref[...] = jnp.broadcast_to(slot, (blocks, LANES))
        for at in range(blocks // LANES):
            square = jnp.broadcast_to(lines[at : at + 1, :], (LANES, LANES))
            inverse_ref[at * LANES : (at + 1) * LANES, :] = 1.0 / jnp.transpose(square)
        for number, table in enumerate(encode_tables(levels_ref)):
            tables_ref[number] = table
        for number, (slope, intercept) in enumerate(line_tables(levels_ref)):
            lines_ref[2 * number] = slope
            lines_ref[2 * number + 1] = intercept

    threshold, slope, intercept = tables_ref[0], tables_ref[1], tables_ref[2]
    deep = 64

    def some_rows(number, carry):
        start = pl.multiple_of(number * deep, deep)
        tiles = [(row, part) for part in range(columns // LANES) for row in range(0, deep, 8)]

        def over(row, part, height=8):
            return pl.ds(pl.multiple_of(start + row, height), height), slice(part * LANES, (part + 1) * LANES)

        ratios = {tile: rotated_ref[over(*tile)] * inverse_ref[over(tile[0], 0)] for tile in tiles}
        by_table = tiles[1::2]
        cells = {tile: (ratios[tile] * CELL_RATE + 32.0).astype(jnp.int32) for tile in by_table}
        limits = {tile: looked_up(threshold, cells[tile]) for tile in by_table}
        sides = {
            tile: jnp.where(ratios[tile] >= limits[tile], cells[tile] + CELLS, cells[tile]) for tile in by_table
        }
        slopes = {tile: looked_up(slope, sides[tile]) for tile in by_table}
        intercepts = {tile: looked_up(intercept, sides[tile]) for tile in by_table}
        values = {}
        for tile in tiles:
            ratio = ratios[tile]
            if tile in slopes:
                value = ratio * slopes[tile] + intercepts[tile]
            else:
                its_slope, its_intercept = lines_ref[0], lines_ref[1]
                for level in range(1, count - 1):
                    above = ratio >= levels_ref[level]
                    its_slope = jnp.where(above, lines_ref[2 * level], its_slope)
                    its_intercept = jnp.where(above, lines_ref[2 * level + 1], its_intercept)
                value = ratio * its_slope + its_intercept
            values[tile] = value + dither_ref[over(*tile)].astype(jnp.float32) * (1.0 / dither_steps)
        for part in range(columns // LANES):
            for row in range(0, deep, 16):
                pair = jnp.concatenate([values[row, part], values[row + 8, part]], axis=0)
                held_ref[over(row, part, 16)] = pair.astype(jnp.bfloat16)
        return carry

    lax.fori_loop(0, blocks // deep, some_rows, 0)
    slotted = jnp.dot(order_ref[...], held_ref[...], preferred_element_type=jnp.float32)

    def copy_out(which):
        there = pl.ds(pl.multiple_of(which * columns, columns), columns)
        slot = which % 2
        return pltpu.make_async_copy(out_ref.at[slot], symbols_ref.at[:, there], out_sems.at[slot])

    @pl.when(step >= 2)
    def _():
        copy_out(step - 2).wait()

    out_ref[step % 2] = slotted.astype(jnp.bfloat16)
    copy_out(step).start()

    @pl.when(step == pl.num_programs(0) - 1)
    def _():
        copy_out(step - 1).wait()
        copy_out(step).wait()


def encode(rotated, dither, peaks, layout, levels):
    blocks, block = rotated.shape
    columns = 1024
    return pl.pallas_call(
        encode_kernel,
        grid=(block // columns,),
        in_specs=[
            pl.BlockSpec(memory_space=pltpu.SMEM),
            pl.BlockSpec((blocks, columns), lambda i: (0, i)),
            pl.BlockSpec((blocks, columns), lambda i: (0, i)),
            pl.BlockSpec(peaks.shape, lambda i: (0, 0, 0)),
            pl.BlockSpec((1, blocks), lambda i: (0, 0)),
        ],
        out_specs=[
            pl.BlockSpec(memory_space=pltpu.HBM),
            pl.BlockSpec((blocks, LANES), lambda i: (0, 0)),
        ],
        out_shape=[
            pltpu.HBM((blocks, block), jnp.bfloat16),
            jax.ShapeDtypeStruct((blocks, LANES), jnp.float32),
        ],
        scratch_shapes=[
            pltpu.VMEM((blocks, LANES), jnp.float32),
            pltpu.VMEM((blocks, blocks), jnp.bfloat16),
            pltpu.VMEM((blocks, columns), jnp.bfloat16),
            pltpu.VMEM((3, 8, LANES), jnp.float32),
            pltpu.VMEM((2 * levels.shape[0], 8, LANES), jnp.float32),
            pltpu.VMEM((2, blocks, columns), jnp.bfloat16),
            pltpu.SemaphoreType.DMA((2,)),
        ],
        compiler_params=pltpu.CompilerParams(vmem_limit_bytes=32 * MIB),
        name="encode",
    )(levels, rotated, dither, peaks, layout)


def owner_kernel(
    place_ref, levels_ref, symbols_ref, scales_ref, bits_ref, master_ref, moment_ref, second_ref,
    new_master_ref, new_moment_ref, new_second_ref, copies_ref, total_ref, table_ref,
):
    step = pl.program_id(0)
    rows, block = total_ref.shape
    replicas, _, columns = symbols_ref.shape
    count = levels_ref.shape[0]

    @pl.when(step == 0)
    def _():
        table = (hadamard(WIDE) * (1.0 / 64.0)).astype(jnp.bfloat16)
        for piece in range(3):
            table_ref[pl.ds(piece * WIDE, WIDE), :] = table

    def column(number, carry):
        here = pl.ds(pl.multiple_of(number * LANES, LANES), LANES)
        there = pl.ds(pl.multiple_of(step * columns + number * LANES, LANES), LANES)
        sums = [jnp.zeros((rows, LANES), jnp.float32) for _ in range(count)]
        for replica in range(replicas):
            symbol = symbols_ref[replica, :, here].astype(jnp.float32)
            for level in range(count):
                sums[level] = sums[level] + jnp.maximum(symbol, float(level))
        total = jnp.full((rows, LANES), levels_ref[0] * float(replicas), jnp.float32)
        for level in range(count - 1):
            spacing = levels_ref[level + 1] - levels_ref[level]
            total = total + spacing * ((sums[level] - sums[level + 1]) + float(replicas))
        total_ref[:, there] = total
        return carry

    lax.fori_loop(0, columns // LANES, column, 0)

    @pl.when(step == pl.num_programs(0) - 1)
    def _():
        flips = (1 - 2 * bits_ref[...]).astype(jnp.float32)
        scales = jnp.concatenate([scales_ref[...]] * (WIDE // LANES), axis=1)
        parts = butterflies(total_ref[:, at : at + WIDE] * scales for at in range(0, block, WIDE))
        turned = times_table(jnp.concatenate(parts, axis=0), table_ref[...])
        for number in range(block // WIDE):
            over = slice(number * WIDE, (number + 1) * WIDE)
            grads = turned[number * rows : (number + 1) * rows] * flips[:, over]
            moment = first_decay * moment_ref[:, over] + (1.0 - first_decay) * grads
            second = second_decay * second_ref[:, over] + (1.0 - second_decay) * grads * grads
            master = master_ref[:, over]
            updated = master - learning_rate * (moment / (jnp.sqrt(second) + adam_epsilon) + weight_decay * master)
            new_moment_ref[:, over] = moment
            new_second_ref[:, over] = second
            new_master_ref[:, over] = updated
            rounded = updated.astype(jnp.bfloat16)
            for copy in range(copies_ref.shape[0]):
                copies_ref[copy, :, over] = rounded


def owner(place, levels, received, scales, bits, master, moment, second, copies):
    replicas, rows, block = received.shape
    columns = 1024
    whole = pl.BlockSpec((rows, block), lambda i, place: (0, 0))
    return pl.pallas_call(
        owner_kernel,
        grid_spec=pltpu.PrefetchScalarGridSpec(
            num_scalar_prefetch=1,
            grid=(block // columns,),
            in_specs=[
                pl.BlockSpec(memory_space=pltpu.SMEM),
                pl.BlockSpec((replicas, rows, columns), lambda i, place: (0, 0, i)),
                pl.BlockSpec((rows, LANES), lambda i, place: (place[0], 0)),
                pl.BlockSpec((1, block), lambda i, place: (0, 0)),
                whole,
                whole,
                whole,
            ],
            out_specs=[whole, whole, whole, pl.BlockSpec((copies, rows, block), lambda i, place: (0, 0, 0))],
            scratch_shapes=[pltpu.VMEM((rows, block), jnp.float32), pltpu.VMEM((3 * WIDE, WIDE), jnp.bfloat16)],
        ),
        out_shape=[jax.ShapeDtypeStruct((rows, block), jnp.float32)] * 3
        + [jax.ShapeDtypeStruct((copies, rows, block), jnp.bfloat16)],
        compiler_params=pltpu.CompilerParams(vmem_limit_bytes=VMEM_BYTES),
        name="owner",
    )(place, levels, received, scales, bits, master, moment, second)


def reorder_kernel(mine_ref, others_ref, my_slots_ref, other_slots_ref, out_ref):
    blocks = out_ref.shape[0]
    half = mine_ref.shape[0]
    row = lax.broadcasted_iota(jnp.int32, (blocks, half), 0)
    my_order = (row == my_slots_ref[...]).astype(jnp.float32).astype(jnp.bfloat16)
    other_order = (row == other_slots_ref[...]).astype(jnp.float32).astype(jnp.bfloat16)
    order = jnp.concatenate([my_order, other_order], axis=1)
    held = jnp.concatenate([mine_ref[...], others_ref[...]], axis=0)
    out_ref[...] = jnp.dot(order, held, preferred_element_type=jnp.float32).astype(jnp.bfloat16)


def reorder(mine, others, my_slots, other_slots):
    half, block = mine.shape
    columns = 1024
    return pl.pallas_call(
        reorder_kernel,
        grid=(block // columns,),
        in_specs=[
            pl.BlockSpec((half, columns), lambda i: (0, i)),
            pl.BlockSpec((half, columns), lambda i: (0, i)),
            pl.BlockSpec((1, half), lambda i: (0, 0)),
            pl.BlockSpec((1, half), lambda i: (0, 0)),
        ],
        out_specs=pl.BlockSpec((2 * half, columns), lambda i: (0, i)),
        out_shape=jax.ShapeDtypeStruct((2 * half, block), jnp.bfloat16),
        compiler_params=pltpu.CompilerParams(vmem_limit_bytes=VMEM_BYTES),
        name="reorder",
    )(mine, others, my_slots, other_slots)


def local(axes, gradient, dither, sign_bits, levels, layout, master, first_moment, second_moment):
    groups = lax.axis_size(axes)
    chips, core = axes[:-1], axes[-1]
    blocks, block = gradient.shape[2:]
    owned = blocks // groups
    bits = sign_bits.reshape(1, block)
    rotated, peaks = rotate(gradient[0, 0], bits, groups)
    peaks = lax.all_to_all(peaks, axes, 0, 0, tiled=True)
    symbols, scales = encode(rotated, dither[0, 0], peaks, layout.reshape(1, blocks), levels)
    received = lax.all_to_all(symbols.reshape(groups, owned, block), axes, 0, 0, tiled=True)
    place = lax.axis_index(axes).reshape(1)
    new_master, new_moment, new_second, copies = owner(
        place, levels, received, scales, bits, master[0], first_moment[0], second_moment[0], groups // 2
    )
    mine = lax.all_to_all(copies, chips, 0, 0, tiled=True)
    others = lax.ppermute(mine, core, OTHER_CORE)
    by_core = layout.reshape(groups // 2, 2, owned)
    which = lax.axis_index(core)
    my_slots = lax.dynamic_index_in_dim(by_core, which, 1, False).reshape(1, blocks // 2)
    other_slots = lax.dynamic_index_in_dim(by_core, 1 - which, 1, False).reshape(1, blocks // 2)
    parameters = reorder(
        mine.reshape(blocks // 2, block), others.reshape(blocks // 2, block), my_slots, other_slots
    )
    return (new_master[None], new_moment[None], new_second[None], parameters[None])


def solution(mesh):
    section, dp = mesh.axis_names
    axes = ("dp_chip", "dp_core")
    split = Mesh(mesh.devices.reshape(mesh.shape[section], mesh.shape[dp] // 2, 2), (section, *axes))
    placed = (
        P(section, axes, None, None),
        P(section, axes, None, None),
        P(),
        P(),
        P(),
        P(section, axes, None),
        P(section, axes, None),
        P(section, axes, None),
    )
    return jax.shard_map(
        functools.partial(local, axes),
        mesh=split,
        in_specs=placed,
        out_specs=(P(section, axes, None), P(section, axes, None), P(section, axes, None), P(section, None, None)),
        check_vma=False,
    )
```

```python
import functools

import jax
import jax.numpy as jnp
from jax import lax
from jax.experimental import pallas as pl
from jax.experimental.pallas import tpu as pltpu
from jax.sharding import Mesh, PartitionSpec as P

adam_epsilon = 1e-08
learning_rate = 0.02
weight_decay = 0.1
first_decay = 0.9
second_decay = 0.95
dither_steps = 256.0

LANES = 128
WIDE = 256
CELLS = 64
CELL_RATE = 31.95
MIB = 1024 * 1024
VMEM_BYTES = 16 * MIB
OTHER_CORE = ((0, 1), (1, 0))


def hadamard(edge):
    common = lax.broadcasted_iota(jnp.int32, (edge, edge), 0) & lax.broadcasted_iota(jnp.int32, (edge, edge), 1)
    parity = jnp.zeros((edge, edge), jnp.int32)
    for bit in range(edge.bit_length() - 1):
        parity = parity ^ ((common >> bit) & 1)
    return (1 - 2 * parity).astype(jnp.float32)


def three_pieces(values):
    high = values.astype(jnp.bfloat16)
    rest = values - high.astype(jnp.float32)
    middle = rest.astype(jnp.bfloat16)
    low = (rest - middle.astype(jnp.float32)).astype(jnp.bfloat16)
    return high, middle, low


def butterflies(parts):
    parts = list(parts)
    stride = 1
    while stride < len(parts):
        for first in range(len(parts)):
            if not first & stride:
                one, two = parts[first], parts[first + stride]
                parts[first], parts[first + stride] = one + two, one - two
        stride *= 2
    return parts


def times_table(values, table):
    pieces = jnp.concatenate(three_pieces(values), axis=1)
    return jnp.dot(pieces, table, preferred_element_type=jnp.float32)


BY_LANE = lax.GatherDimensionNumbers(
    offset_dims=(),
    collapsed_slice_dims=(1,),
    start_index_map=(1,),
    operand_batching_dims=(0,),
    start_indices_batching_dims=(0,),
)


def looked_up(table, index):
    return lax.gather(table, index[..., None], BY_LANE, (1, 1), mode=lax.GatherScatterMode.PROMISE_IN_BOUNDS)


def rotate_kernel(gradient_ref, bits_ref, rotated_ref, peaks_ref, table_ref, rows_ref):
    step = pl.program_id(0)
    rows, block = gradient_ref.shape

    @pl.when(step == 0)
    def _():
        table = (hadamard(WIDE) * (1.0 / 64.0)).astype(jnp.bfloat16)
        for piece in range(3):
            table_ref[pl.ds(piece * WIDE, WIDE), :] = table

    flips = (1 - 2 * bits_ref[...]).astype(jnp.float32)
    parts = butterflies(gradient_ref[:, at : at + WIDE] * flips[:, at : at + WIDE] for at in range(0, block, WIDE))
    turned = times_table(jnp.concatenate(parts, axis=0), table_ref[...])
    most = jnp.zeros((rows, WIDE), jnp.float32)
    for number in range(block // WIDE):
        part = turned[number * rows : (number + 1) * rows]
        rotated_ref[:, number * WIDE : (number + 1) * WIDE] = part
        most = jnp.maximum(most, jnp.abs(part))
    rows_ref[pl.ds(pl.multiple_of(step * rows, rows), rows), :] = jnp.maximum(most[:, :LANES], most[:, LANES:])

    @pl.when(step == pl.num_programs(0) - 1)
    def _():
        blocks = rows_ref.shape[0]
        lines = [
            jnp.max(jnp.transpose(rows_ref[at : at + LANES, :]), axis=0, keepdims=True) for at in range(0, blocks, LANES)
        ]
        lines = jnp.concatenate(lines * (8 // len(lines)), axis=0)
        peaks_ref[...] = jnp.broadcast_to(lines[None], peaks_ref.shape)


def rotate(gradient, bits, groups):
    blocks, block = gradient.shape
    rows = 64
    return pl.pallas_call(
        rotate_kernel,
        grid=(blocks // rows,),
        in_specs=[
            pl.BlockSpec((rows, block), lambda i: (i, 0)),
            pl.BlockSpec((1, block), lambda i: (0, 0)),
        ],
        out_specs=[
            pl.BlockSpec((rows, block), lambda i: (i, 0)),
            pl.BlockSpec((groups, 8, LANES), lambda i: (0, 0, 0)),
        ],
        out_shape=[
            jax.ShapeDtypeStruct((blocks, block), jnp.float32),
            jax.ShapeDtypeStruct((groups, 8, LANES), jnp.float32),
        ],
        scratch_shapes=[pltpu.VMEM((3 * WIDE, WIDE), jnp.bfloat16), pltpu.VMEM((blocks, LANES), jnp.float32)],
        compiler_params=pltpu.CompilerParams(vmem_limit_bytes=49 * MIB),
        name="rotate",
    )(gradient, bits)


def encode_tables(levels_ref):
    count = levels_ref.shape[0]
    lane = lax.broadcasted_iota(jnp.int32, (8, LANES), 1)
    cell = lane & (CELLS - 1)
    threshold = jnp.full((8, LANES), 4.0, jnp.float32)
    position = jnp.zeros((8, LANES), jnp.int32)
    for number in range(1, count - 1):
        level = jnp.full((8, LANES), levels_ref[number], jnp.float32)
        its_cell = (level * CELL_RATE + 32.0).astype(jnp.int32)
        threshold = jnp.where(its_cell == cell, level, threshold)
        before = (its_cell < cell) | ((its_cell == cell) & (lane >= CELLS))
        position = position + before.astype(jnp.int32)
    slope = jnp.zeros((8, LANES), jnp.float32)
    intercept = jnp.zeros((8, LANES), jnp.float32)
    for number in range(count - 1):
        low = jnp.full((8, LANES), levels_ref[number], jnp.float32)
        high = jnp.full((8, LANES), levels_ref[number + 1], jnp.float32)
        its_slope = 1.0 / (high - low)
        its_intercept = (number + (0.5 / dither_steps - 0.5)) - low * its_slope
        slope = jnp.where(position == number, its_slope, slope)
        intercept = jnp.where(position == number, its_intercept, intercept)
    return threshold, slope, intercept


def line_tables(levels_ref):
    lines = []
    for number in range(levels_ref.shape[0] - 1):
        low = jnp.full((8, LANES), levels_ref[number], jnp.float32)
        slope = 1.0 / (jnp.full((8, LANES), levels_ref[number + 1], jnp.float32) - low)
        lines.append((slope, (number + (0.5 / dither_steps - 0.5)) - low * slope))
    return lines


def encode_kernel(
    levels_ref, rotated_ref, dither_ref, peaks_ref, layout_ref, symbols_ref, scales_ref,
    inverse_ref, order_ref, held_ref, tables_ref, lines_ref, out_ref, out_sems,
):
    step = pl.program_id(0)
    blocks = rotated_ref.shape[0]
    columns = held_ref.shape[1]
    count = levels_ref.shape[0]

    @pl.when(step == 0)
    def _():
        lines = jnp.max(peaks_ref[...], axis=0) + 1e-06
        wide = jnp.concatenate([lines[i : i + 1, :] for i in range(blocks // LANES)], axis=1)
        order = lax.broadcasted_iota(jnp.int32, (blocks, blocks), 0) == layout_ref[...]
        order = jnp.transpose(order.astype(jnp.float32))
        order_ref[...] = order.astype(jnp.bfloat16)
        slot = jnp.sum(jnp.where(order > 0.5, wide, 0.0), axis=1, keepdims=True)
        scales_ref[...] = jnp.broadcast_to(slot, (blocks, LANES))
        for at in range(blocks // LANES):
            square = jnp.broadcast_to(lines[at : at + 1, :], (LANES, LANES))
            inverse_ref[at * LANES : (at + 1) * LANES, :] = 1.0 / jnp.transpose(square)
        for number, table in enumerate(encode_tables(levels_ref)):
            tables_ref[number] = table
        for number, (slope, intercept) in enumerate(line_tables(levels_ref)):
            lines_ref[2 * number] = slope
            lines_ref[2 * number + 1] = intercept

    threshold, slope, intercept = tables_ref[0], tables_ref[1], tables_ref[2]
    deep = 128

    def some_rows(number, carry):
        start = pl.multiple_of(number * deep, deep)
        tiles = [(row, part) for part in range(columns // LANES) for row in range(0, deep, 8)]

        def over(row, part, height=8):
            return pl.ds(pl.multiple_of(start + row, height), height), slice(part * LANES, (part + 1) * LANES)

        def whole(row, part):
            return pl.ds(pl.multiple_of(start + row, 8), 8), pl.ds(pl.multiple_of(step * columns + part * LANES, LANES), LANES)

        ratios = {tile: rotated_ref[whole(*tile)] * inverse_ref[over(tile[0], 0)] for tile in tiles}
        by_table = tiles[1::2]
        cells = {tile: (ratios[tile] * CELL_RATE + 32.0).astype(jnp.int32) for tile in by_table}
        limits = {tile: looked_up(threshold, cells[tile]) for tile in by_table}
        sides = {
            tile: jnp.where(ratios[tile] >= limits[tile], cells[tile] + CELLS, cells[tile]) for tile in by_table
        }
        slopes = {tile: looked_up(slope, sides[tile]) for tile in by_table}
        intercepts = {tile: looked_up(intercept, sides[tile]) for tile in by_table}
        values = {}
        for tile in tiles:
            ratio = ratios[tile]
            if tile in slopes:
                value = ratio * slopes[tile] + intercepts[tile]
            else:
                its_slope, its_intercept = lines_ref[0], lines_ref[1]
                for level in range(1, count - 1):
                    above = ratio >= levels_ref[level]
                    its_slope = jnp.where(above, lines_ref[2 * level], its_slope)
                    its_intercept = jnp.where(above, lines_ref[2 * level + 1], its_intercept)
                value = ratio * its_slope + its_intercept
            values[tile] = value + dither_ref[whole(*tile)].astype(jnp.float32) * (1.0 / dither_steps)
        for part in range(columns // LANES):
            for row in range(0, deep, 16):
                pair = jnp.concatenate([values[row, part], values[row + 8, part]], axis=0)
                held_ref[over(row, part, 16)] = pair.astype(jnp.bfloat16)
        return carry

    lax.fori_loop(0, blocks // deep, some_rows, 0)
    slotted = jnp.dot(order_ref[...], held_ref[...], preferred_element_type=jnp.float32)

    def copy_out(which):
        there = pl.ds(pl.multiple_of(which * columns, columns), columns)
        slot = which % 2
        return pltpu.make_async_copy(out_ref.at[slot], symbols_ref.at[:, there], out_sems.at[slot])

    @pl.when(step >= 2)
    def _():
        copy_out(step - 2).wait()

    out_ref[step % 2] = slotted.astype(jnp.bfloat16)
    copy_out(step).start()

    @pl.when(step == pl.num_programs(0) - 1)
    def _():
        copy_out(step - 1).wait()
        copy_out(step).wait()


def encode(rotated, dither, peaks, layout, levels):
    blocks, block = rotated.shape
    columns = 1024
    return pl.pallas_call(
        encode_kernel,
        grid=(block // columns,),
        in_specs=[
            pl.BlockSpec(memory_space=pltpu.SMEM),
            pl.BlockSpec(memory_space=pltpu.VMEM),
            pl.BlockSpec(memory_space=pltpu.VMEM),
            pl.BlockSpec(peaks.shape, lambda i: (0, 0, 0)),
            pl.BlockSpec((1, blocks), lambda i: (0, 0)),
        ],
        out_specs=[
            pl.BlockSpec(memory_space=pltpu.HBM),
            pl.BlockSpec((blocks, LANES), lambda i: (0, 0)),
        ],
        out_shape=[
            pltpu.HBM((blocks, block), jnp.bfloat16),
            jax.ShapeDtypeStruct((blocks, LANES), jnp.float32),
        ],
        scratch_shapes=[
            pltpu.VMEM((blocks, LANES), jnp.float32),
            pltpu.VMEM((blocks, blocks), jnp.bfloat16),
            pltpu.VMEM((blocks, columns), jnp.bfloat16),
            pltpu.VMEM((3, 8, LANES), jnp.float32),
            pltpu.VMEM((2 * levels.shape[0], 8, LANES), jnp.float32),
            pltpu.VMEM((2, blocks, columns), jnp.bfloat16),
            pltpu.SemaphoreType.DMA((2,)),
        ],
        compiler_params=pltpu.CompilerParams(vmem_limit_bytes=32 * MIB),
        name="encode",
    )(levels, rotated, dither, peaks, layout)


def owner_kernel(
    place_ref, levels_ref, symbols_ref, scales_ref, bits_ref, master_ref, moment_ref, second_ref,
    new_master_ref, new_moment_ref, new_second_ref, copies_ref, total_ref, table_ref,
):
    step = pl.program_id(0)
    rows, block = total_ref.shape
    replicas = symbols_ref.shape[0]
    columns = block // pl.num_programs(0)
    count = levels_ref.shape[0]

    @pl.when(step == 0)
    def _():
        table = (hadamard(WIDE) * (1.0 / 64.0)).astype(jnp.bfloat16)
        for piece in range(3):
            table_ref[pl.ds(piece * WIDE, WIDE), :] = table

    def column(number, carry):
        there = pl.ds(pl.multiple_of(step * columns + number * LANES, LANES), LANES)
        sums = [jnp.zeros((rows, LANES), jnp.float32) for _ in range(count)]
        for replica in range(replicas):
            symbol = symbols_ref[replica, :, there].astype(jnp.float32)
            for level in range(count):
                sums[level] = sums[level] + jnp.maximum(symbol, float(level))
        total = jnp.full((rows, LANES), levels_ref[0] * float(replicas), jnp.float32)
        for level in range(count - 1):
            spacing = levels_ref[level + 1] - levels_ref[level]
            total = total + spacing * ((sums[level] - sums[level + 1]) + float(replicas))
        total_ref[:, there] = total
        return carry

    lax.fori_loop(0, columns // LANES, column, 0)

    @pl.when(step == pl.num_programs(0) - 1)
    def _():
        flips = (1 - 2 * bits_ref[...]).astype(jnp.float32)
        scales = jnp.concatenate([scales_ref[...]] * (WIDE // LANES), axis=1)
        parts = butterflies(total_ref[:, at : at + WIDE] * scales for at in range(0, block, WIDE))
        turned = times_table(jnp.concatenate(parts, axis=0), table_ref[...])
        for number in range(block // WIDE):
            over = slice(number * WIDE, (number + 1) * WIDE)
            grads = turned[number * rows : (number + 1) * rows] * flips[:, over]
            moment = first_decay * moment_ref[:, over] + (1.0 - first_decay) * grads
            second = second_decay * second_ref[:, over] + (1.0 - second_decay) * grads * grads
            master = master_ref[:, over]
            updated = master - learning_rate * (moment / (jnp.sqrt(second) + adam_epsilon) + weight_decay * master)
            new_moment_ref[:, over] = moment
            new_second_ref[:, over] = second
            new_master_ref[:, over] = updated
            rounded = updated.astype(jnp.bfloat16)
            for copy in range(copies_ref.shape[0]):
                copies_ref[copy, :, over] = rounded


def owner(place, levels, received, scales, bits, master, moment, second, copies):
    replicas, rows, block = received.shape
    columns = block
    whole = pl.BlockSpec((rows, block), lambda i, place: (0, 0))
    return pl.pallas_call(
        owner_kernel,
        grid_spec=pltpu.PrefetchScalarGridSpec(
            num_scalar_prefetch=1,
            grid=(block // columns,),
            in_specs=[
                pl.BlockSpec(memory_space=pltpu.SMEM),
                pl.BlockSpec(memory_space=pltpu.VMEM),
                pl.BlockSpec((rows, LANES), lambda i, place: (place[0], 0)),
                pl.BlockSpec((1, block), lambda i, place: (0, 0)),
                whole,
                whole,
                whole,
            ],
            out_specs=[whole, whole, whole, pl.BlockSpec((copies, rows, block), lambda i, place: (0, 0, 0))],
            scratch_shapes=[pltpu.VMEM((rows, block), jnp.float32), pltpu.VMEM((3 * WIDE, WIDE), jnp.bfloat16)],
        ),
        out_shape=[jax.ShapeDtypeStruct((rows, block), jnp.float32)] * 3
        + [jax.ShapeDtypeStruct((copies, rows, block), jnp.bfloat16)],
        compiler_params=pltpu.CompilerParams(vmem_limit_bytes=VMEM_BYTES),
        name="owner",
    )(place, levels, received, scales, bits, master, moment, second)


def reorder_kernel(mine_ref, others_ref, my_slots_ref, other_slots_ref, out_ref):
    blocks = out_ref.shape[0]
    half = mine_ref.shape[0]
    row = lax.broadcasted_iota(jnp.int32, (blocks, half), 0)
    my_order = (row == my_slots_ref[...]).astype(jnp.float32).astype(jnp.bfloat16)
    other_order = (row == other_slots_ref[...]).astype(jnp.float32).astype(jnp.bfloat16)
    order = jnp.concatenate([my_order, other_order], axis=1)
    here = pl.ds(pl.multiple_of(pl.program_id(0) * out_ref.shape[1], LANES), out_ref.shape[1])
    held = jnp.concatenate([mine_ref[:, here], others_ref[:, here]], axis=0)
    out_ref[...] = jnp.dot(order, held, preferred_element_type=jnp.float32).astype(jnp.bfloat16)


def reorder(mine, others, my_slots, other_slots):
    half, block = mine.shape
    columns = 1024
    return pl.pallas_call(
        reorder_kernel,
        grid=(block // columns,),
        in_specs=[
            pl.BlockSpec(memory_space=pltpu.VMEM),
            pl.BlockSpec(memory_space=pltpu.VMEM),
            pl.BlockSpec((1, half), lambda i: (0, 0)),
            pl.BlockSpec((1, half), lambda i: (0, 0)),
        ],
        out_specs=pl.BlockSpec((2 * half, columns), lambda i: (0, i)),
        out_shape=jax.ShapeDtypeStruct((2 * half, block), jnp.bfloat16),
        compiler_params=pltpu.CompilerParams(vmem_limit_bytes=VMEM_BYTES),
        name="reorder",
    )(mine, others, my_slots, other_slots)


def local(axes, gradient, dither, sign_bits, levels, layout, master, first_moment, second_moment):
    groups = lax.axis_size(axes)
    chips, core = axes[:-1], axes[-1]
    blocks, block = gradient.shape[2:]
    owned = blocks // groups
    bits = sign_bits.reshape(1, block)
    rotated, peaks = rotate(gradient[0, 0], pltpu.with_memory_space_constraint(bits, pltpu.HBM), groups)
    dither, rotated, peaks = lax.optimization_barrier((dither, rotated, peaks))
    peaks = lax.all_to_all(peaks, axes, 0, 0, tiled=True)
    symbols, scales = encode(rotated, dither[0, 0], peaks, layout.reshape(1, blocks), levels)
    received = lax.all_to_all(symbols.reshape(groups, owned, block), axes, 0, 0, tiled=True)
    place = lax.axis_index(axes).reshape(1)
    new_master, new_moment, new_second, copies = owner(
        place, levels, received, scales, bits, master[0], first_moment[0], second_moment[0], groups // 2
    )
    mine = lax.all_to_all(copies, chips, 0, 0, tiled=True)
    others = lax.ppermute(mine, core, OTHER_CORE)
    by_core = layout.reshape(groups // 2, 2, owned)
    which = lax.axis_index(core)
    my_slots = lax.dynamic_index_in_dim(by_core, which, 1, False).reshape(1, blocks // 2)
    other_slots = lax.dynamic_index_in_dim(by_core, 1 - which, 1, False).reshape(1, blocks // 2)
    parameters = reorder(
        mine.reshape(blocks // 2, block), others.reshape(blocks // 2, block), my_slots, other_slots
    )
    return (new_master[None], new_moment[None], new_second[None], parameters[None])


def solution(mesh):
    section, dp = mesh.axis_names
    axes = ("dp_chip", "dp_core")
    split = Mesh(mesh.devices.reshape(mesh.shape[section], mesh.shape[dp] // 2, 2), (section, *axes))
    placed = (
        P(section, axes, None, None),
        P(section, axes, None, None),
        P(),
        P(),
        P(),
        P(section, axes, None),
        P(section, axes, None),
        P(section, axes, None),
    )
    return jax.shard_map(
        functools.partial(local, axes),
        mesh=split,
        in_specs=placed,
        out_specs=(P(section, axes, None), P(section, axes, None), P(section, axes, None), P(section, None, None)),
        check_vma=False,
    )
```

```python
import functools

import jax
import jax.numpy as jnp
from jax import lax
from jax.experimental import pallas as pl
from jax.experimental.pallas import tpu as pltpu
from jax.sharding import Mesh, PartitionSpec as P

adam_epsilon = 1e-08
learning_rate = 0.02
weight_decay = 0.1
first_decay = 0.9
second_decay = 0.95
dither_steps = 256.0

LANES = 128
WIDE = 256
CELLS = 64
CELL_RATE = 31.95
MIB = 1024 * 1024
VMEM_BYTES = 16 * MIB
OTHER_CORE = ((0, 1), (1, 0))


def hadamard(edge):
    common = lax.broadcasted_iota(jnp.int32, (edge, edge), 0) & lax.broadcasted_iota(jnp.int32, (edge, edge), 1)
    parity = jnp.zeros((edge, edge), jnp.int32)
    for bit in range(edge.bit_length() - 1):
        parity = parity ^ ((common >> bit) & 1)
    return (1 - 2 * parity).astype(jnp.float32)


def three_pieces(values):
    high = values.astype(jnp.bfloat16)
    rest = values - high.astype(jnp.float32)
    middle = rest.astype(jnp.bfloat16)
    low = (rest - middle.astype(jnp.float32)).astype(jnp.bfloat16)
    return high, middle, low


def butterflies(parts):
    parts = list(parts)
    stride = 1
    while stride < len(parts):
        for first in range(len(parts)):
            if not first & stride:
                one, two = parts[first], parts[first + stride]
                parts[first], parts[first + stride] = one + two, one - two
        stride *= 2
    return parts


def times_table(values, table):
    pieces = jnp.concatenate(three_pieces(values), axis=1)
    return jnp.dot(pieces, table, preferred_element_type=jnp.float32)


BY_LANE = lax.GatherDimensionNumbers(
    offset_dims=(),
    collapsed_slice_dims=(1,),
    start_index_map=(1,),
    operand_batching_dims=(0,),
    start_indices_batching_dims=(0,),
)


def looked_up(table, index):
    return lax.gather(table, index[..., None], BY_LANE, (1, 1), mode=lax.GatherScatterMode.PROMISE_IN_BOUNDS)


def rotate_kernel(gradient_ref, bits_ref, rotated_ref, peaks_ref, table_ref, rows_ref):
    step = pl.program_id(0)
    rows, block = gradient_ref.shape

    @pl.when(step == 0)
    def _():
        table = (hadamard(WIDE) * (1.0 / 64.0)).astype(jnp.bfloat16)
        for piece in range(3):
            table_ref[pl.ds(piece * WIDE, WIDE), :] = table

    flips = (1 - 2 * bits_ref[...]).astype(jnp.float32)
    parts = butterflies(gradient_ref[:, at : at + WIDE] * flips[:, at : at + WIDE] for at in range(0, block, WIDE))
    turned = times_table(jnp.concatenate(parts, axis=0), table_ref[...])
    most = jnp.zeros((rows, WIDE), jnp.float32)
    for number in range(block // WIDE):
        part = turned[number * rows : (number + 1) * rows]
        rotated_ref[:, number * WIDE : (number + 1) * WIDE] = part
        most = jnp.maximum(most, jnp.abs(part))
    rows_ref[pl.ds(pl.multiple_of(step * rows, rows), rows), :] = jnp.maximum(most[:, :LANES], most[:, LANES:])

    @pl.when(step == pl.num_programs(0) - 1)
    def _():
        blocks = rows_ref.shape[0]
        lines = [
            jnp.max(jnp.transpose(rows_ref[at : at + LANES, :]), axis=0, keepdims=True) for at in range(0, blocks, LANES)
        ]
        lines = jnp.concatenate(lines * (8 // len(lines)), axis=0)
        peaks_ref[...] = jnp.broadcast_to(lines[None], peaks_ref.shape)


def rotate(gradient, bits, groups):
    blocks, block = gradient.shape
    rows = 64
    return pl.pallas_call(
        rotate_kernel,
        grid=(blocks // rows,),
        in_specs=[
            pl.BlockSpec((rows, block), lambda i: (i, 0)),
            pl.BlockSpec((1, block), lambda i: (0, 0)),
        ],
        out_specs=[
            pl.BlockSpec((rows, block), lambda i: (i, 0)),
            pl.BlockSpec((groups, 8, LANES), lambda i: (0, 0, 0)),
        ],
        out_shape=[
            jax.ShapeDtypeStruct((blocks, block), jnp.float32),
            jax.ShapeDtypeStruct((groups, 8, LANES), jnp.float32),
        ],
        scratch_shapes=[pltpu.VMEM((3 * WIDE, WIDE), jnp.bfloat16), pltpu.VMEM((blocks, LANES), jnp.float32)],
        compiler_params=pltpu.CompilerParams(vmem_limit_bytes=49 * MIB),
        name="rotate",
    )(gradient, bits)


def encode_tables(levels_ref):
    count = levels_ref.shape[0]
    lane = lax.broadcasted_iota(jnp.int32, (8, LANES), 1)
    cell = lane & (CELLS - 1)
    threshold = jnp.full((8, LANES), 4.0, jnp.float32)
    position = jnp.zeros((8, LANES), jnp.int32)
    for number in range(1, count - 1):
        level = jnp.full((8, LANES), levels_ref[number], jnp.float32)
        its_cell = (level * CELL_RATE + 32.0).astype(jnp.int32)
        threshold = jnp.where(its_cell == cell, level, threshold)
        before = (its_cell < cell) | ((its_cell == cell) & (lane >= CELLS))
        position = position + before.astype(jnp.int32)
    slope = jnp.zeros((8, LANES), jnp.float32)
    intercept = jnp.zeros((8, LANES), jnp.float32)
    for number in range(count - 1):
        low = jnp.full((8, LANES), levels_ref[number], jnp.float32)
        high = jnp.full((8, LANES), levels_ref[number + 1], jnp.float32)
        its_slope = 1.0 / (high - low)
        its_intercept = (number + (0.5 / dither_steps - 0.5)) - low * its_slope
        slope = jnp.where(position == number, its_slope, slope)
        intercept = jnp.where(position == number, its_intercept, intercept)
    return threshold, slope, intercept


def line_tables(levels_ref):
    lines = []
    for number in range(levels_ref.shape[0] - 1):
        low = jnp.full((8, LANES), levels_ref[number], jnp.float32)
        slope = 1.0 / (jnp.full((8, LANES), levels_ref[number + 1], jnp.float32) - low)
        lines.append((slope, (number + (0.5 / dither_steps - 0.5)) - low * slope))
    return lines


def encode_kernel(
    core, levels_ref, rotated_ref, dither_ref, peaks_ref, layout_ref, mine_ref, others_ref, scales_ref,
    inverse_ref, order_ref, held_ref, tables_ref, lines_ref,
):
    step = pl.program_id(0)
    blocks = rotated_ref.shape[0]
    columns = held_ref.shape[1]
    count = levels_ref.shape[0]

    @pl.when(step == 0)
    def _():
        lines = jnp.max(peaks_ref[...], axis=0) + 1e-06
        wide = jnp.concatenate([lines[i : i + 1, :] for i in range(blocks // LANES)], axis=1)
        order = lax.broadcasted_iota(jnp.int32, (blocks, blocks), 0) == layout_ref[...]
        order = jnp.transpose(order.astype(jnp.float32))
        by_core = order.reshape(blocks // 16, 2, 8, blocks)
        first, second = by_core[:, 0].reshape(blocks // 2, blocks), by_core[:, 1].reshape(blocks // 2, blocks)
        is_first = lax.axis_index(core) == 0
        grouped = [jnp.where(is_first, first, second), jnp.where(is_first, second, first)]
        order_ref[...] = jnp.concatenate(grouped, axis=0).astype(jnp.bfloat16)
        slot = jnp.sum(jnp.where(order > 0.5, wide, 0.0), axis=1, keepdims=True)
        scales_ref[...] = jnp.broadcast_to(slot, (blocks, LANES))
        for at in range(blocks // LANES):
            square = jnp.broadcast_to(lines[at : at + 1, :], (LANES, LANES))
            inverse_ref[at * LANES : (at + 1) * LANES, :] = 1.0 / jnp.transpose(square)
        for number, table in enumerate(encode_tables(levels_ref)):
            tables_ref[number] = table
        for number, (slope, intercept) in enumerate(line_tables(levels_ref)):
            lines_ref[2 * number] = slope
            lines_ref[2 * number + 1] = intercept

    threshold, slope, intercept = tables_ref[0], tables_ref[1], tables_ref[2]
    deep = 128

    def some_rows(number, carry):
        start = pl.multiple_of(number * deep, deep)
        tiles = [(row, part) for part in range(columns // LANES) for row in range(0, deep, 8)]

        def over(row, part, height=8):
            return pl.ds(pl.multiple_of(start + row, height), height), slice(part * LANES, (part + 1) * LANES)

        def whole(row, part):
            return pl.ds(pl.multiple_of(start + row, 8), 8), pl.ds(pl.multiple_of(step * columns + part * LANES, LANES), LANES)

        ratios = {tile: rotated_ref[whole(*tile)] * inverse_ref[over(tile[0], 0)] for tile in tiles}
        by_table = tiles[1::2]
        cells = {tile: (ratios[tile] * CELL_RATE + 32.0).astype(jnp.int32) for tile in by_table}
        limits = {tile: looked_up(threshold, cells[tile]) for tile in by_table}
        sides = {
            tile: jnp.where(ratios[tile] >= limits[tile], cells[tile] + CELLS, cells[tile]) for tile in by_table
        }
        slopes = {tile: looked_up(slope, sides[tile]) for tile in by_table}
        intercepts = {tile: looked_up(intercept, sides[tile]) for tile in by_table}
        values = {}
        for tile in tiles:
            ratio = ratios[tile]
            if tile in slopes:
                value = ratio * slopes[tile] + intercepts[tile]
            else:
                its_slope, its_intercept = lines_ref[0], lines_ref[1]
                for level in range(1, count - 1):
                    above = ratio >= levels_ref[level]
                    its_slope = jnp.where(above, lines_ref[2 * level], its_slope)
                    its_intercept = jnp.where(above, lines_ref[2 * level + 1], its_intercept)
                value = ratio * its_slope + its_intercept
            values[tile] = value + dither_ref[whole(*tile)].astype(jnp.float32) * (1.0 / dither_steps)
        for part in range(columns // LANES):
            for row in range(0, deep, 16):
                pair = jnp.concatenate([values[row, part], values[row + 8, part]], axis=0)
                held_ref[over(row, part, 16)] = pair.astype(jnp.bfloat16)
        return carry

    lax.fori_loop(0, blocks // deep, some_rows, 0)
    slotted = jnp.dot(order_ref[...], held_ref[...], preferred_element_type=jnp.float32)

    there = pl.ds(pl.multiple_of(step * columns, columns), columns)
    mine_ref[:, there] = slotted[: blocks // 2].astype(jnp.bfloat16)
    others_ref[:, there] = slotted[blocks // 2 :].astype(jnp.bfloat16)


def encode(core, rotated, dither, peaks, layout, levels):
    blocks, block = rotated.shape
    columns = 1024
    return pl.pallas_call(
        functools.partial(encode_kernel, core),
        grid=(block // columns,),
        in_specs=[
            pl.BlockSpec(memory_space=pltpu.SMEM),
            pl.BlockSpec(memory_space=pltpu.VMEM),
            pl.BlockSpec(memory_space=pltpu.VMEM),
            pl.BlockSpec(peaks.shape, lambda i: (0, 0, 0)),
            pl.BlockSpec((1, blocks), lambda i: (0, 0)),
        ],
        out_specs=[
            pl.BlockSpec(memory_space=pltpu.VMEM),
            pl.BlockSpec(memory_space=pltpu.VMEM),
            pl.BlockSpec((blocks, LANES), lambda i: (0, 0)),
        ],
        out_shape=[
            pltpu.VMEM((blocks // 2, block), jnp.bfloat16),
            pltpu.VMEM((blocks // 2, block), jnp.bfloat16),
            jax.ShapeDtypeStruct((blocks, LANES), jnp.float32),
        ],
        scratch_shapes=[
            pltpu.VMEM((blocks, LANES), jnp.float32),
            pltpu.VMEM((blocks, blocks), jnp.bfloat16),
            pltpu.VMEM((blocks, columns), jnp.bfloat16),
            pltpu.VMEM((3, 8, LANES), jnp.float32),
            pltpu.VMEM((2 * levels.shape[0], 8, LANES), jnp.float32),
        ],
        compiler_params=pltpu.CompilerParams(vmem_limit_bytes=32 * MIB),
        name="encode",
    )(levels, rotated, dither, peaks, layout)


def merge_kernel(levels_ref, mine_ref, theirs_ref, out_ref):
    count = levels_ref.shape[0]
    rows, block = out_ref.shape
    wide = 1024
    spacings = [levels_ref[level + 1] - levels_ref[level] for level in range(count - 1)]
    weights = [spacings[0]] + [spacings[level] - spacings[level - 1] for level in range(1, count - 1)] + [-spacings[-1]]

    def some(number, carry):
        here = pl.ds(pl.multiple_of(number // (block // wide) * 16, 16), 16)
        start = number % (block // wide) * wide
        for part in range(wide // LANES):
            there = pl.ds(pl.multiple_of(start + part * LANES, LANES), LANES)
            one, two = mine_ref[here, there].astype(jnp.float32), theirs_ref[here, there].astype(jnp.float32)
            total = jnp.full((16, LANES), 2.0 * levels_ref[count - 1], jnp.float32)
            for level in range(count):
                total = total + weights[level] * (jnp.maximum(one, float(level)) + jnp.maximum(two, float(level)))
            out_ref[here, there] = total
        return carry

    lax.fori_loop(0, rows // 16 * (block // wide), some, 0)


def merge(levels, mine, theirs):
    here = pl.BlockSpec(memory_space=pltpu.VMEM)
    return pl.pallas_call(
        merge_kernel,
        in_specs=[pl.BlockSpec(memory_space=pltpu.SMEM), here, here],
        out_specs=here,
        out_shape=pltpu.VMEM(mine.shape, jnp.float32),
        compiler_params=pltpu.CompilerParams(vmem_limit_bytes=VMEM_BYTES),
        name="merge",
    )(levels, mine, theirs)


def owner_kernel(
    place_ref, total_ref, scales_ref, bits_ref, master_ref, moment_ref, second_ref,
    new_master_ref, new_moment_ref, new_second_ref, copies_ref, table_ref,
):
    rows, block = total_ref.shape
    table = (hadamard(WIDE) * (1.0 / 64.0)).astype(jnp.bfloat16)
    for piece in range(3):
        table_ref[pl.ds(piece * WIDE, WIDE), :] = table
    flips = (1 - 2 * bits_ref[...]).astype(jnp.float32)
    scales = jnp.concatenate([scales_ref[...]] * (WIDE // LANES), axis=1)
    parts = butterflies(total_ref[:, at : at + WIDE] * scales for at in range(0, block, WIDE))
    turned = times_table(jnp.concatenate(parts, axis=0), table_ref[...])
    for number in range(block // WIDE):
        over = slice(number * WIDE, (number + 1) * WIDE)
        grads = turned[number * rows : (number + 1) * rows] * flips[:, over]
        moment = first_decay * moment_ref[:, over] + (1.0 - first_decay) * grads
        second = second_decay * second_ref[:, over] + (1.0 - second_decay) * grads * grads
        master = master_ref[:, over]
        updated = master - learning_rate * (moment / (jnp.sqrt(second) + adam_epsilon) + weight_decay * master)
        new_moment_ref[:, over] = moment
        new_second_ref[:, over] = second
        new_master_ref[:, over] = updated
        rounded = updated.astype(jnp.bfloat16)
        for copy in range(copies_ref.shape[0]):
            copies_ref[copy, :, over] = rounded


def owner(place, total, scales, bits, master, moment, second, copies):
    rows, block = total.shape
    whole = pl.BlockSpec((rows, block), lambda i, place: (0, 0))
    return pl.pallas_call(
        owner_kernel,
        grid_spec=pltpu.PrefetchScalarGridSpec(
            num_scalar_prefetch=1,
            grid=(1,),
            in_specs=[
                whole,
                pl.BlockSpec((rows, LANES), lambda i, place: (place[0], 0)),
                pl.BlockSpec((1, block), lambda i, place: (0, 0)),
                whole,
                whole,
                whole,
            ],
            out_specs=[whole, whole, whole, pl.BlockSpec((copies, rows, block), lambda i, place: (0, 0, 0))],
            scratch_shapes=[pltpu.VMEM((3 * WIDE, WIDE), jnp.bfloat16)],
        ),
        out_shape=[jax.ShapeDtypeStruct((rows, block), jnp.float32)] * 3
        + [jax.ShapeDtypeStruct((copies, rows, block), jnp.bfloat16)],
        compiler_params=pltpu.CompilerParams(vmem_limit_bytes=VMEM_BYTES),
        name="owner",
    )(place, total, scales, bits, master, moment, second)


def reorder_kernel(mine_ref, others_ref, my_slots_ref, other_slots_ref, out_ref):
    blocks = out_ref.shape[0]
    half = mine_ref.shape[0]
    row = lax.broadcasted_iota(jnp.int32, (blocks, half), 0)
    my_order = (row == my_slots_ref[...]).astype(jnp.float32).astype(jnp.bfloat16)
    other_order = (row == other_slots_ref[...]).astype(jnp.float32).astype(jnp.bfloat16)
    order = jnp.concatenate([my_order, other_order], axis=1)
    here = pl.ds(pl.multiple_of(pl.program_id(0) * out_ref.shape[1], LANES), out_ref.shape[1])
    held = jnp.concatenate([mine_ref[:, here], others_ref[:, here]], axis=0)
    out_ref[...] = jnp.dot(order, held, preferred_element_type=jnp.float32).astype(jnp.bfloat16)


def reorder(mine, others, my_slots, other_slots):
    half, block = mine.shape
    columns = 1024
    return pl.pallas_call(
        reorder_kernel,
        grid=(block // columns,),
        in_specs=[
            pl.BlockSpec(memory_space=pltpu.VMEM),
            pl.BlockSpec(memory_space=pltpu.VMEM),
            pl.BlockSpec((1, half), lambda i: (0, 0)),
            pl.BlockSpec((1, half), lambda i: (0, 0)),
        ],
        out_specs=pl.BlockSpec((2 * half, columns), lambda i: (0, i)),
        out_shape=jax.ShapeDtypeStruct((2 * half, block), jnp.bfloat16),
        compiler_params=pltpu.CompilerParams(vmem_limit_bytes=VMEM_BYTES),
        name="reorder",
    )(mine, others, my_slots, other_slots)


def local(axes, gradient, dither, sign_bits, levels, layout, master, first_moment, second_moment):
    groups = lax.axis_size(axes)
    chips, core = axes[:-1], axes[-1]
    blocks, block = gradient.shape[2:]
    owned = blocks // groups
    bits = sign_bits.reshape(1, block)
    rotated, peaks = rotate(gradient[0, 0], pltpu.with_memory_space_constraint(bits, pltpu.HBM), groups)
    dither, rotated, peaks = lax.optimization_barrier((dither, rotated, peaks))
    peaks = lax.all_to_all(peaks, axes, 0, 0, tiled=True)
    mine, others, scales = encode(core, rotated, dither[0, 0], peaks, layout.reshape(1, blocks), levels)
    merged = merge(levels, mine, lax.ppermute(others, core, OTHER_CORE))
    pairs = merged.astype(jnp.float16).reshape(groups // 2, owned, block)
    pairs = lax.all_to_all(pairs, chips, 0, 0, tiled=True)
    total = jnp.sum(pairs.astype(jnp.float32), axis=0)
    place = lax.axis_index(axes).reshape(1)
    new_master, new_moment, new_second, copies = owner(
        place, total, scales, bits, master[0], first_moment[0], second_moment[0], groups // 2
    )
    mine = lax.all_to_all(copies, chips, 0, 0, tiled=True)
    others = lax.ppermute(mine, core, OTHER_CORE)
    by_core = layout.reshape(groups // 2, 2, owned)
    which = lax.axis_index(core)
    my_slots = lax.dynamic_index_in_dim(by_core, which, 1, False).reshape(1, blocks // 2)
    other_slots = lax.dynamic_index_in_dim(by_core, 1 - which, 1, False).reshape(1, blocks // 2)
    parameters = reorder(
        mine.reshape(blocks // 2, block), others.reshape(blocks // 2, block), my_slots, other_slots
    )
    return (new_master[None], new_moment[None], new_second[None], parameters[None])


def solution(mesh):
    section, dp = mesh.axis_names
    axes = ("dp_chip", "dp_core")
    split = Mesh(mesh.devices.reshape(mesh.shape[section], mesh.shape[dp] // 2, 2), (section, *axes))
    placed = (
        P(section, axes, None, None),
        P(section, axes, None, None),
        P(),
        P(),
        P(),
        P(section, axes, None),
        P(section, axes, None),
        P(section, axes, None),
    )
    return jax.shard_map(
        functools.partial(local, axes),
        mesh=split,
        in_specs=placed,
        out_specs=(P(section, axes, None), P(section, axes, None), P(section, axes, None), P(section, None, None)),
        check_vma=False,
    )
```

```python
import functools

import jax
import jax.numpy as jnp
from jax import lax
from jax.experimental import pallas as pl
from jax.experimental.pallas import tpu as pltpu
from jax.sharding import Mesh, PartitionSpec as P

adam_epsilon = 1e-08
learning_rate = 0.02
weight_decay = 0.1
first_decay = 0.9
second_decay = 0.95
dither_steps = 256.0

LANES = 128
WIDE = 256
CELLS = 64
CELL_RATE = 31.95
MIB = 1024 * 1024
TABLE_EVERY = 2
VMEM_BYTES = 16 * MIB
OTHER_CORE = ((0, 1), (1, 0))


def hadamard(edge):
    common = lax.broadcasted_iota(jnp.int32, (edge, edge), 0) & lax.broadcasted_iota(jnp.int32, (edge, edge), 1)
    parity = jnp.zeros((edge, edge), jnp.int32)
    for bit in range(edge.bit_length() - 1):
        parity = parity ^ ((common >> bit) & 1)
    return (1 - 2 * parity).astype(jnp.float32)


def three_pieces(values):
    high = values.astype(jnp.bfloat16)
    rest = values - high.astype(jnp.float32)
    middle = rest.astype(jnp.bfloat16)
    low = (rest - middle.astype(jnp.float32)).astype(jnp.bfloat16)
    return high, middle, low


def butterflies(parts):
    parts = list(parts)
    stride = 1
    while stride < len(parts):
        for first in range(len(parts)):
            if not first & stride:
                one, two = parts[first], parts[first + stride]
                parts[first], parts[first + stride] = one + two, one - two
        stride *= 2
    return parts


def times_table(values, table):
    pieces = jnp.concatenate(three_pieces(values), axis=1)
    return jnp.dot(pieces, table, preferred_element_type=jnp.float32)


BY_LANE = lax.GatherDimensionNumbers(
    offset_dims=(),
    collapsed_slice_dims=(1,),
    start_index_map=(1,),
    operand_batching_dims=(0,),
    start_indices_batching_dims=(0,),
)


def looked_up(table, index):
    return lax.gather(table, index[..., None], BY_LANE, (1, 1), mode=lax.GatherScatterMode.PROMISE_IN_BOUNDS)


def rotate_kernel(gradient_ref, bits_ref, rotated_ref, peaks_ref, table_ref, rows_ref):
    step = pl.program_id(0)
    rows, block = gradient_ref.shape

    @pl.when(step == 0)
    def _():
        table = (hadamard(WIDE) * (1.0 / 64.0)).astype(jnp.bfloat16)
        for piece in range(3):
            table_ref[pl.ds(piece * WIDE, WIDE), :] = table

    flips = (1 - 2 * bits_ref[...]).astype(jnp.float32)
    parts = butterflies(gradient_ref[:, at : at + WIDE] * flips[:, at : at + WIDE] for at in range(0, block, WIDE))
    turned = times_table(jnp.concatenate(parts, axis=0), table_ref[...])
    most = jnp.zeros((rows, WIDE), jnp.float32)
    for number in range(block // WIDE):
        part = turned[number * rows : (number + 1) * rows]
        rotated_ref[:, number * WIDE : (number + 1) * WIDE] = part
        most = jnp.maximum(most, jnp.abs(part))
    rows_ref[pl.ds(pl.multiple_of(step * rows, rows), rows), :] = jnp.maximum(most[:, :LANES], most[:, LANES:])

    @pl.when(step == pl.num_programs(0) - 1)
    def _():
        blocks = rows_ref.shape[0]
        lines = [
            jnp.max(jnp.transpose(rows_ref[at : at + LANES, :]), axis=0, keepdims=True) for at in range(0, blocks, LANES)
        ]
        lines = jnp.concatenate(lines * (8 // len(lines)), axis=0)
        peaks_ref[...] = jnp.broadcast_to(lines[None], peaks_ref.shape)


def rotate(gradient, bits, groups):
    blocks, block = gradient.shape
    rows = 64
    return pl.pallas_call(
        rotate_kernel,
        grid=(blocks // rows,),
        in_specs=[
            pl.BlockSpec((rows, block), lambda i: (i, 0)),
            pl.BlockSpec((1, block), lambda i: (0, 0)),
        ],
        out_specs=[
            pl.BlockSpec((rows, block), lambda i: (i, 0)),
            pl.BlockSpec((groups, 8, LANES), lambda i: (0, 0, 0)),
        ],
        out_shape=[
            jax.ShapeDtypeStruct((blocks, block), jnp.float32),
            jax.ShapeDtypeStruct((groups, 8, LANES), jnp.float32),
        ],
        scratch_shapes=[pltpu.VMEM((3 * WIDE, WIDE), jnp.bfloat16), pltpu.VMEM((blocks, LANES), jnp.float32)],
        compiler_params=pltpu.CompilerParams(vmem_limit_bytes=49 * MIB),
        name="rotate",
    )(gradient, bits)


def encode_tables(levels_ref):
    count = levels_ref.shape[0]
    lane = lax.broadcasted_iota(jnp.int32, (8, LANES), 1)
    cell = lane & (CELLS - 1)
    threshold = jnp.full((8, LANES), 4.0, jnp.float32)
    position = jnp.zeros((8, LANES), jnp.int32)
    for number in range(1, count - 1):
        level = jnp.full((8, LANES), levels_ref[number], jnp.float32)
        its_cell = (level * CELL_RATE + 32.0).astype(jnp.int32)
        threshold = jnp.where(its_cell == cell, level, threshold)
        before = (its_cell < cell) | ((its_cell == cell) & (lane >= CELLS))
        position = position + before.astype(jnp.int32)
    slope = jnp.zeros((8, LANES), jnp.float32)
    intercept = jnp.zeros((8, LANES), jnp.float32)
    for number in range(count - 1):
        low = jnp.full((8, LANES), levels_ref[number], jnp.float32)
        high = jnp.full((8, LANES), levels_ref[number + 1], jnp.float32)
        its_slope = 1.0 / (high - low)
        its_intercept = (number + (0.5 / dither_steps - 0.5)) - low * its_slope
        slope = jnp.where(position == number, its_slope, slope)
        intercept = jnp.where(position == number, its_intercept, intercept)
    return threshold, slope, intercept


def line_tables(levels_ref):
    lines = []
    for number in range(levels_ref.shape[0] - 1):
        low = jnp.full((8, LANES), levels_ref[number], jnp.float32)
        slope = 1.0 / (jnp.full((8, LANES), levels_ref[number + 1], jnp.float32) - low)
        lines.append((slope, (number + (0.5 / dither_steps - 0.5)) - low * slope))
    return lines


def encode_kernel(
    core, levels_ref, rotated_ref, dither_ref, peaks_ref, layout_ref, mine_ref, others_ref, scales_ref,
    inverse_ref, order_ref, held_ref, tables_ref, lines_ref,
):
    step = pl.program_id(0)
    blocks = rotated_ref.shape[0]
    columns = held_ref.shape[1]
    count = levels_ref.shape[0]

    @pl.when(step == 0)
    def _():
        lines = jnp.max(peaks_ref[...], axis=0) + 1e-06
        wide = jnp.concatenate([lines[i : i + 1, :] for i in range(blocks // LANES)], axis=1)
        order = lax.broadcasted_iota(jnp.int32, (blocks, blocks), 0) == layout_ref[...]
        order = jnp.transpose(order.astype(jnp.float32))
        by_core = order.reshape(blocks // 16, 2, 8, blocks)
        first, second = by_core[:, 0].reshape(blocks // 2, blocks), by_core[:, 1].reshape(blocks // 2, blocks)
        is_first = lax.axis_index(core) == 0
        grouped = [jnp.where(is_first, first, second), jnp.where(is_first, second, first)]
        order_ref[...] = jnp.concatenate(grouped, axis=0).astype(jnp.bfloat16)
        slot = jnp.sum(jnp.where(order > 0.5, wide, 0.0), axis=1, keepdims=True)
        scales_ref[...] = jnp.broadcast_to(slot, (blocks, LANES))
        for at in range(blocks // LANES):
            square = jnp.broadcast_to(lines[at : at + 1, :], (LANES, LANES))
            inverse_ref[at * LANES : (at + 1) * LANES, :] = 1.0 / jnp.transpose(square)
        for number, table in enumerate(encode_tables(levels_ref)):
            tables_ref[number] = table
        for number, (slope, intercept) in enumerate(line_tables(levels_ref)):
            lines_ref[2 * number] = slope
            lines_ref[2 * number + 1] = intercept

    threshold, slope, intercept = tables_ref[0], tables_ref[1], tables_ref[2]
    deep = 128

    def some_rows(number, carry):
        start = pl.multiple_of(number * deep, deep)
        tiles = [(row, part) for part in range(columns // LANES) for row in range(0, deep, 8)]

        def over(row, part, height=8):
            return pl.ds(pl.multiple_of(start + row, height), height), slice(part * LANES, (part + 1) * LANES)

        def whole(row, part):
            return pl.ds(pl.multiple_of(start + row, 8), 8), pl.ds(pl.multiple_of(step * columns + part * LANES, LANES), LANES)

        ratios = {tile: rotated_ref[whole(*tile)] * inverse_ref[over(tile[0], 0)] for tile in tiles}
        by_table = tiles[1::2]
        cells = {tile: (ratios[tile] * CELL_RATE + 32.0).astype(jnp.int32) for tile in by_table}
        limits = {tile: looked_up(threshold, cells[tile]) for tile in by_table}
        sides = {
            tile: jnp.where(ratios[tile] >= limits[tile], cells[tile] + CELLS, cells[tile]) for tile in by_table
        }
        slopes = {tile: looked_up(slope, sides[tile]) for tile in by_table}
        intercepts = {tile: looked_up(intercept, sides[tile]) for tile in by_table}
        values = {}
        for tile in tiles:
            ratio = ratios[tile]
            if tile in slopes:
                value = ratio * slopes[tile] + intercepts[tile]
            else:
                its_slope, its_intercept = lines_ref[0], lines_ref[1]
                for level in range(1, count - 1):
                    above = ratio >= levels_ref[level]
                    its_slope = jnp.where(above, lines_ref[2 * level], its_slope)
                    its_intercept = jnp.where(above, lines_ref[2 * level + 1], its_intercept)
                value = ratio * its_slope + its_intercept
            values[tile] = value + dither_ref[whole(*tile)].astype(jnp.float32) * (1.0 / dither_steps)
        for part in range(columns // LANES):
            for row in range(0, deep, 16):
                pair = jnp.concatenate([values[row, part], values[row + 8, part]], axis=0)
                held_ref[over(row, part, 16)] = pair.astype(jnp.bfloat16)
        return carry

    lax.fori_loop(0, blocks // deep, some_rows, 0)
    slotted = jnp.dot(order_ref[...], held_ref[...], preferred_element_type=jnp.float32)

    there = pl.ds(pl.multiple_of(step * columns, columns), columns)
    mine_ref[:, there] = slotted[: blocks // 2].astype(jnp.bfloat16)
    others_ref[:, there] = slotted[blocks // 2 :].astype(jnp.bfloat16)


def encode(core, rotated, dither, peaks, layout, levels):
    blocks, block = rotated.shape
    columns = 1024
    return pl.pallas_call(
        functools.partial(encode_kernel, core),
        grid=(block // columns,),
        in_specs=[
            pl.BlockSpec(memory_space=pltpu.SMEM),
            pl.BlockSpec(memory_space=pltpu.VMEM),
            pl.BlockSpec(memory_space=pltpu.VMEM),
            pl.BlockSpec(peaks.shape, lambda i: (0, 0, 0)),
            pl.BlockSpec((1, blocks), lambda i: (0, 0)),
        ],
        out_specs=[
            pl.BlockSpec(memory_space=pltpu.VMEM),
            pl.BlockSpec(memory_space=pltpu.VMEM),
            pl.BlockSpec((blocks, LANES), lambda i: (0, 0)),
        ],
        out_shape=[
            pltpu.VMEM((blocks // 2, block), jnp.bfloat16),
            pltpu.VMEM((blocks // 2, block), jnp.bfloat16),
            jax.ShapeDtypeStruct((blocks, LANES), jnp.float32),
        ],
        scratch_shapes=[
            pltpu.VMEM((blocks, LANES), jnp.float32),
            pltpu.VMEM((blocks, blocks), jnp.bfloat16),
            pltpu.VMEM((blocks, columns), jnp.bfloat16),
            pltpu.VMEM((3, 8, LANES), jnp.float32),
            pltpu.VMEM((2 * levels.shape[0], 8, LANES), jnp.float32),
        ],
        compiler_params=pltpu.CompilerParams(vmem_limit_bytes=32 * MIB),
        name="encode",
    )(levels, rotated, dither, peaks, layout)


def decode_tables(levels_ref):
    count = levels_ref.shape[0]
    lane = lax.broadcasted_iota(jnp.int32, (8, LANES), 1)
    slope = jnp.zeros((8, LANES), jnp.float32)
    intercept = jnp.full((8, LANES), levels_ref[count - 1], jnp.float32)
    for number in range(count - 1):
        low = jnp.full((8, LANES), levels_ref[number], jnp.float32)
        spacing = jnp.full((8, LANES), levels_ref[number + 1], jnp.float32) - low
        slope = jnp.where(lane == number, spacing, slope)
        intercept = jnp.where(lane == number, low - number * spacing, intercept)
    return slope, intercept


def decode_kernel(levels_ref, symbols_ref, *refs):
    out_ref = refs[-1]
    count = levels_ref.shape[0]
    rows, block = out_ref.shape
    wide, deep = 1024, 64
    slope, intercept = decode_tables(levels_ref)
    spacings = [levels_ref[level + 1] - levels_ref[level] for level in range(count - 1)]
    weights = [spacings[0]] + [spacings[level] - spacings[level - 1] for level in range(1, count - 1)] + [-spacings[-1]]

    def some(number, carry):
        down = pl.multiple_of(number // (block // wide) * deep, deep)
        start = number % (block // wide) * wide
        places, tiles = [], []
        for part in range(wide // LANES):
            for row in range(0, deep, 16):
                place = (
                    pl.ds(pl.multiple_of(down + row, 16), 16),
                    pl.ds(pl.multiple_of(start + part * LANES, LANES), LANES),
                )
                symbols = symbols_ref[place].astype(jnp.float32)
                places.append(place)
                tiles += [symbols[:8], symbols[8:]]
        by_table = [at % TABLE_EVERY == 1 for at in range(len(tiles))]
        bounded = {
            at: jnp.minimum(jnp.maximum(tile, 0.0), count - 1.0) for at, tile in enumerate(tiles) if by_table[at]
        }
        index = {at: tile.astype(jnp.int32) for at, tile in bounded.items()}
        lines = {at: (looked_up(slope, which), looked_up(intercept, which)) for at, which in index.items()}
        values = []
        for at, tile in enumerate(tiles):
            if by_table[at]:
                value = bounded[at] * lines[at][0] + lines[at][1]
            else:
                value = jnp.full((8, LANES), levels_ref[count - 1], jnp.float32)
                for level in range(count):
                    value = value + weights[level] * jnp.maximum(tile, float(level))
            values.append(value)
        for at, place in enumerate(places):
            value = jnp.concatenate(values[2 * at : 2 * at + 2], axis=0)
            for ref in refs[:-1]:
                value = value + ref[place]
            out_ref[place] = value
        return carry

    lax.fori_loop(0, rows // deep * (block // wide), some, 0)


def decode(levels, symbols, *others):
    here = pl.BlockSpec(memory_space=pltpu.VMEM)
    return pl.pallas_call(
        decode_kernel,
        in_specs=[pl.BlockSpec(memory_space=pltpu.SMEM), here] + [here] * len(others),
        out_specs=here,
        out_shape=pltpu.VMEM(symbols.shape, jnp.float32),
        compiler_params=pltpu.CompilerParams(vmem_limit_bytes=VMEM_BYTES),
        cost_estimate=pl.CostEstimate(flops=48 * symbols.size, bytes_accessed=6 * symbols.size, transcendentals=0),
        name="decode",
    )(levels, symbols, *others)


def owner_kernel(
    place_ref, total_ref, scales_ref, bits_ref, master_ref, moment_ref, second_ref,
    new_master_ref, new_moment_ref, new_second_ref, copies_ref, table_ref,
):
    rows, block = total_ref.shape
    table = (hadamard(WIDE) * (1.0 / 64.0)).astype(jnp.bfloat16)
    for piece in range(3):
        table_ref[pl.ds(piece * WIDE, WIDE), :] = table
    flips = (1 - 2 * bits_ref[...]).astype(jnp.float32)
    scales = jnp.concatenate([scales_ref[...]] * (WIDE // LANES), axis=1)
    parts = butterflies(total_ref[:, at : at + WIDE] * scales for at in range(0, block, WIDE))
    turned = times_table(jnp.concatenate(parts, axis=0), table_ref[...])
    for number in range(block // WIDE):
        over = slice(number * WIDE, (number + 1) * WIDE)
        grads = turned[number * rows : (number + 1) * rows] * flips[:, over]
        moment = first_decay * moment_ref[:, over] + (1.0 - first_decay) * grads
        second = second_decay * second_ref[:, over] + (1.0 - second_decay) * grads * grads
        master = master_ref[:, over]
        updated = master - learning_rate * (moment / (jnp.sqrt(second) + adam_epsilon) + weight_decay * master)
        new_moment_ref[:, over] = moment
        new_second_ref[:, over] = second
        new_master_ref[:, over] = updated
        rounded = updated.astype(jnp.bfloat16)
        for copy in range(copies_ref.shape[0]):
            copies_ref[copy, :, over] = rounded


def owner(place, total, scales, bits, master, moment, second, copies):
    rows, block = total.shape
    whole = pl.BlockSpec((rows, block), lambda i, place: (0, 0))
    return pl.pallas_call(
        owner_kernel,
        grid_spec=pltpu.PrefetchScalarGridSpec(
            num_scalar_prefetch=1,
            grid=(1,),
            in_specs=[
                whole,
                pl.BlockSpec((rows, LANES), lambda i, place: (place[0], 0)),
                pl.BlockSpec((1, block), lambda i, place: (0, 0)),
                whole,
                whole,
                whole,
            ],
            out_specs=[whole, whole, whole, pl.BlockSpec((copies, rows, block), lambda i, place: (0, 0, 0))],
            scratch_shapes=[pltpu.VMEM((3 * WIDE, WIDE), jnp.bfloat16)],
        ),
        out_shape=[jax.ShapeDtypeStruct((rows, block), jnp.float32)] * 3
        + [jax.ShapeDtypeStruct((copies, rows, block), jnp.bfloat16)],
        compiler_params=pltpu.CompilerParams(vmem_limit_bytes=VMEM_BYTES),
        name="owner",
    )(place, total, scales, bits, master, moment, second)


def reorder_kernel(mine_ref, others_ref, my_slots_ref, other_slots_ref, out_ref):
    blocks = out_ref.shape[0]
    half = mine_ref.shape[0]
    row = lax.broadcasted_iota(jnp.int32, (blocks, half), 0)
    my_order = (row == my_slots_ref[...]).astype(jnp.float32).astype(jnp.bfloat16)
    other_order = (row == other_slots_ref[...]).astype(jnp.float32).astype(jnp.bfloat16)
    order = jnp.concatenate([my_order, other_order], axis=1)
    here = pl.ds(pl.multiple_of(pl.program_id(0) * out_ref.shape[1], LANES), out_ref.shape[1])
    held = jnp.concatenate([mine_ref[:, here], others_ref[:, here]], axis=0)
    out_ref[...] = jnp.dot(order, held, preferred_element_type=jnp.float32).astype(jnp.bfloat16)


def reorder(mine, others, my_slots, other_slots):
    half, block = mine.shape
    columns = 1024
    return pl.pallas_call(
        reorder_kernel,
        grid=(block // columns,),
        in_specs=[
            pl.BlockSpec(memory_space=pltpu.VMEM),
            pl.BlockSpec(memory_space=pltpu.VMEM),
            pl.BlockSpec((1, half), lambda i: (0, 0)),
            pl.BlockSpec((1, half), lambda i: (0, 0)),
        ],
        out_specs=pl.BlockSpec((2 * half, columns), lambda i: (0, i)),
        out_shape=jax.ShapeDtypeStruct((2 * half, block), jnp.bfloat16),
        compiler_params=pltpu.CompilerParams(vmem_limit_bytes=VMEM_BYTES),
        name="reorder",
    )(mine, others, my_slots, other_slots)


def local(axes, gradient, dither, sign_bits, levels, layout, master, first_moment, second_moment):
    groups = lax.axis_size(axes)
    chips, core = axes[:-1], axes[-1]
    blocks, block = gradient.shape[2:]
    owned = blocks // groups
    bits = sign_bits.reshape(1, block)
    rotated, peaks = rotate(gradient[0, 0], pltpu.with_memory_space_constraint(bits, pltpu.HBM), groups)
    dither, rotated, peaks = lax.optimization_barrier((dither, rotated, peaks))
    peaks = lax.all_to_all(peaks, axes, 0, 0, tiled=True)
    mine, others, scales = encode(core, rotated, dither[0, 0], peaks, layout.reshape(1, blocks), levels)
    theirs = lax.ppermute(others, core, OTHER_CORE)
    merged = decode(levels, theirs, decode(levels, mine))
    pairs = merged.astype(jnp.float16).reshape(groups // 2, owned, block)
    pairs = lax.all_to_all(pairs, chips, 0, 0, tiled=True)
    total = jnp.sum(pairs.astype(jnp.float32), axis=0)
    place = lax.axis_index(axes).reshape(1)
    new_master, new_moment, new_second, copies = owner(
        place, total, scales, bits, master[0], first_moment[0], second_moment[0], groups // 2
    )
    mine = lax.all_to_all(copies, chips, 0, 0, tiled=True)
    others = lax.ppermute(mine, core, OTHER_CORE)
    by_core = layout.reshape(groups // 2, 2, owned)
    which = lax.axis_index(core)
    my_slots = lax.dynamic_index_in_dim(by_core, which, 1, False).reshape(1, blocks // 2)
    other_slots = lax.dynamic_index_in_dim(by_core, 1 - which, 1, False).reshape(1, blocks // 2)
    parameters = reorder(
        mine.reshape(blocks // 2, block), others.reshape(blocks // 2, block), my_slots, other_slots
    )
    return (new_master[None], new_moment[None], new_second[None], parameters[None])


def solution(mesh):
    section, dp = mesh.axis_names
    axes = ("dp_chip", "dp_core")
    split = Mesh(mesh.devices.reshape(mesh.shape[section], mesh.shape[dp] // 2, 2), (section, *axes))
    placed = (
        P(section, axes, None, None),
        P(section, axes, None, None),
        P(),
        P(),
        P(),
        P(section, axes, None),
        P(section, axes, None),
        P(section, axes, None),
    )
    return jax.shard_map(
        functools.partial(local, axes),
        mesh=split,
        in_specs=placed,
        out_specs=(P(section, axes, None), P(section, axes, None), P(section, axes, None), P(section, None, None)),
        check_vma=False,
    )
```

```python
import functools

import jax
import jax.numpy as jnp
from jax import lax
from jax.experimental import pallas as pl
from jax.experimental.pallas import tpu as pltpu
from jax.sharding import Mesh, PartitionSpec as P

adam_epsilon = 1e-08
learning_rate = 0.02
weight_decay = 0.1
first_decay = 0.9
second_decay = 0.95
dither_steps = 256.0

LANES = 128
WIDE = 256
CELLS = 64
CELL_RATE = 31.95
MIB = 1024 * 1024
TABLE_EVERY = 2
VMEM_BYTES = 16 * MIB
OTHER_CORE = ((0, 1), (1, 0))


def hadamard(edge):
    common = lax.broadcasted_iota(jnp.int32, (edge, edge), 0) & lax.broadcasted_iota(jnp.int32, (edge, edge), 1)
    parity = jnp.zeros((edge, edge), jnp.int32)
    for bit in range(edge.bit_length() - 1):
        parity = parity ^ ((common >> bit) & 1)
    return (1 - 2 * parity).astype(jnp.float32)


def three_pieces(values):
    high = values.astype(jnp.bfloat16)
    rest = values - high.astype(jnp.float32)
    middle = rest.astype(jnp.bfloat16)
    low = (rest - middle.astype(jnp.float32)).astype(jnp.bfloat16)
    return high, middle, low


def butterflies(parts):
    parts = list(parts)
    stride = 1
    while stride < len(parts):
        for first in range(len(parts)):
            if not first & stride:
                one, two = parts[first], parts[first + stride]
                parts[first], parts[first + stride] = one + two, one - two
        stride *= 2
    return parts


def times_table(values, table):
    pieces = jnp.concatenate(three_pieces(values), axis=1)
    return jnp.dot(pieces, table, preferred_element_type=jnp.float32)


BY_LANE = lax.GatherDimensionNumbers(
    offset_dims=(),
    collapsed_slice_dims=(1,),
    start_index_map=(1,),
    operand_batching_dims=(0,),
    start_indices_batching_dims=(0,),
)


def looked_up(table, index):
    return lax.gather(table, index[..., None], BY_LANE, (1, 1), mode=lax.GatherScatterMode.PROMISE_IN_BOUNDS)


def rotate_kernel(gradient_ref, bits_ref, rotated_ref, peaks_ref, table_ref, rows_ref):
    step = pl.program_id(0)
    rows, block = gradient_ref.shape

    @pl.when(step == 0)
    def _():
        table = (hadamard(WIDE) * (1.0 / 64.0)).astype(jnp.bfloat16)
        for piece in range(3):
            table_ref[pl.ds(piece * WIDE, WIDE), :] = table

    flips = (1 - 2 * bits_ref[...]).astype(jnp.float32)
    parts = butterflies(gradient_ref[:, at : at + WIDE] * flips[:, at : at + WIDE] for at in range(0, block, WIDE))
    turned = times_table(jnp.concatenate(parts, axis=0), table_ref[...])
    most = jnp.zeros((rows, WIDE), jnp.float32)
    for number in range(block // WIDE):
        part = turned[number * rows : (number + 1) * rows]
        rotated_ref[:, number * WIDE : (number + 1) * WIDE] = part
        most = jnp.maximum(most, jnp.abs(part))
    rows_ref[pl.ds(pl.multiple_of(step * rows, rows), rows), :] = jnp.maximum(most[:, :LANES], most[:, LANES:])

    @pl.when(step == pl.num_programs(0) - 1)
    def _():
        blocks = rows_ref.shape[0]
        lines = [
            jnp.max(jnp.transpose(rows_ref[at : at + LANES, :]), axis=0, keepdims=True) for at in range(0, blocks, LANES)
        ]
        lines = jnp.concatenate(lines, axis=0)
        peaks_ref[...] = jnp.broadcast_to(lines[None], peaks_ref.shape)


def rotate(gradient, bits, groups):
    blocks, block = gradient.shape
    rows = 128
    return pl.pallas_call(
        rotate_kernel,
        grid=(blocks // rows,),
        in_specs=[
            pl.BlockSpec((rows, block), lambda i: (i, 0)),
            pl.BlockSpec((1, block), lambda i: (0, 0)),
        ],
        out_specs=[
            pl.BlockSpec((rows, block), lambda i: (i, 0)),
            pl.BlockSpec((groups, blocks // LANES, LANES), lambda i: (0, 0, 0)),
        ],
        out_shape=[
            jax.ShapeDtypeStruct((blocks, block), jnp.float32),
            jax.ShapeDtypeStruct((groups, blocks // LANES, LANES), jnp.float32),
        ],
        scratch_shapes=[pltpu.VMEM((3 * WIDE, WIDE), jnp.bfloat16), pltpu.VMEM((blocks, LANES), jnp.float32)],
        compiler_params=pltpu.CompilerParams(vmem_limit_bytes=49 * MIB),
        name="rotate",
    )(gradient, bits)


def encode_tables(levels_ref):
    count = levels_ref.shape[0]
    lane = lax.broadcasted_iota(jnp.int32, (8, LANES), 1)
    cell = lane & (CELLS - 1)
    threshold = jnp.full((8, LANES), 4.0, jnp.float32)
    position = jnp.zeros((8, LANES), jnp.int32)
    for number in range(1, count - 1):
        level = jnp.full((8, LANES), levels_ref[number], jnp.float32)
        its_cell = (level * CELL_RATE + 32.0).astype(jnp.int32)
        threshold = jnp.where(its_cell == cell, level, threshold)
        before = (its_cell < cell) | ((its_cell == cell) & (lane >= CELLS))
        position = position + before.astype(jnp.int32)
    slope = jnp.zeros((8, LANES), jnp.float32)
    intercept = jnp.zeros((8, LANES), jnp.float32)
    for number in range(count - 1):
        low = jnp.full((8, LANES), levels_ref[number], jnp.float32)
        high = jnp.full((8, LANES), levels_ref[number + 1], jnp.float32)
        its_slope = 1.0 / (high - low)
        its_intercept = (number + (0.5 / dither_steps - 0.5)) - low * its_slope
        slope = jnp.where(position == number, its_slope, slope)
        intercept = jnp.where(position == number, its_intercept, intercept)
    return threshold, slope, intercept


def line_tables(levels_ref):
    lines = []
    for number in range(levels_ref.shape[0] - 1):
        low = jnp.full((8, LANES), levels_ref[number], jnp.float32)
        slope = 1.0 / (jnp.full((8, LANES), levels_ref[number + 1], jnp.float32) - low)
        lines.append((slope, (number + (0.5 / dither_steps - 0.5)) - low * slope))
    return lines


def encode_kernel(
    core, levels_ref, rotated_ref, dither_ref, peaks_ref, layout_ref, mine_ref, others_ref, scales_ref,
    inverse_ref, order_ref, held_ref, tables_ref, lines_ref,
):
    step = pl.program_id(0)
    blocks = rotated_ref.shape[0]
    columns = held_ref.shape[1]
    count = levels_ref.shape[0]

    @pl.when(step == 0)
    def _():
        lines = jnp.max(peaks_ref[...], axis=0) + 1e-06
        wide = jnp.concatenate([lines[i : i + 1, :] for i in range(blocks // LANES)], axis=1)
        order = lax.broadcasted_iota(jnp.int32, (blocks, blocks), 0) == layout_ref[...]
        order = jnp.transpose(order.astype(jnp.float32))
        by_core = order.reshape(blocks // 16, 2, 8, blocks)
        first, second = by_core[:, 0].reshape(blocks // 2, blocks), by_core[:, 1].reshape(blocks // 2, blocks)
        is_first = lax.axis_index(core) == 0
        grouped = [jnp.where(is_first, first, second), jnp.where(is_first, second, first)]
        order_ref[...] = jnp.concatenate(grouped, axis=0).astype(jnp.bfloat16)
        slot = jnp.sum(jnp.where(order > 0.5, wide, 0.0), axis=1, keepdims=True)
        scales_ref[...] = jnp.broadcast_to(slot, (blocks, LANES))
        for at in range(blocks // LANES):
            square = jnp.broadcast_to(lines[at : at + 1, :], (LANES, LANES))
            inverse_ref[at * LANES : (at + 1) * LANES, :] = 1.0 / jnp.transpose(square)
        for number, table in enumerate(encode_tables(levels_ref)):
            tables_ref[number] = table
        for number, (slope, intercept) in enumerate(line_tables(levels_ref)):
            lines_ref[2 * number] = slope
            lines_ref[2 * number + 1] = intercept

    threshold, slope, intercept = tables_ref[0], tables_ref[1], tables_ref[2]
    deep = 64

    def some_rows(number, carry):
        start = pl.multiple_of(number * deep, deep)
        tiles = [(row, part) for part in range(columns // LANES) for row in range(0, deep, 8)]

        def over(row, part, height=8):
            return pl.ds(pl.multiple_of(start + row, height), height), slice(part * LANES, (part + 1) * LANES)

        def whole(row, part):
            return pl.ds(pl.multiple_of(start + row, 8), 8), pl.ds(pl.multiple_of(step * columns + part * LANES, LANES), LANES)

        ratios = {tile: rotated_ref[whole(*tile)] * inverse_ref[over(tile[0], 0)] for tile in tiles}
        by_table = tiles[1::2]
        cells = {tile: (ratios[tile] * CELL_RATE + 32.0).astype(jnp.int32) for tile in by_table}
        limits = {tile: looked_up(threshold, cells[tile]) for tile in by_table}
        sides = {
            tile: jnp.where(ratios[tile] >= limits[tile], cells[tile] + CELLS, cells[tile]) for tile in by_table
        }
        slopes = {tile: looked_up(slope, sides[tile]) for tile in by_table}
        intercepts = {tile: looked_up(intercept, sides[tile]) for tile in by_table}
        values = {}
        for tile in tiles:
            ratio = ratios[tile]
            if tile in slopes:
                value = ratio * slopes[tile] + intercepts[tile]
            else:
                its_slope, its_intercept = lines_ref[0], lines_ref[1]
                for level in range(1, count - 1):
                    above = ratio >= levels_ref[level]
                    its_slope = jnp.where(above, lines_ref[2 * level], its_slope)
                    its_intercept = jnp.where(above, lines_ref[2 * level + 1], its_intercept)
                value = ratio * its_slope + its_intercept
            values[tile] = value + dither_ref[whole(*tile)].astype(jnp.float32) * (1.0 / dither_steps)
        for part in range(columns // LANES):
            for row in range(0, deep, 16):
                pair = jnp.concatenate([values[row, part], values[row + 8, part]], axis=0)
                held_ref[over(row, part, 16)] = pair.astype(jnp.bfloat16)
        return carry

    lax.fori_loop(0, blocks // deep, some_rows, 0)
    slotted = jnp.dot(order_ref[...], held_ref[...], preferred_element_type=jnp.float32)

    there = pl.ds(pl.multiple_of(step * columns, columns), columns)
    mine_ref[:, there] = slotted[: blocks // 2].astype(jnp.bfloat16)
    others_ref[:, there] = slotted[blocks // 2 :].astype(jnp.bfloat16)


def encode(core, rotated, dither, peaks, layout, levels):
    blocks, block = rotated.shape
    columns = 2048
    return pl.pallas_call(
        functools.partial(encode_kernel, core),
        grid=(block // columns,),
        in_specs=[
            pl.BlockSpec(memory_space=pltpu.SMEM),
            pl.BlockSpec(memory_space=pltpu.VMEM),
            pl.BlockSpec(memory_space=pltpu.VMEM),
            pl.BlockSpec(peaks.shape, lambda i: (0, 0, 0)),
            pl.BlockSpec((1, blocks), lambda i: (0, 0)),
        ],
        out_specs=[
            pl.BlockSpec(memory_space=pltpu.VMEM),
            pl.BlockSpec(memory_space=pltpu.VMEM),
            pl.BlockSpec((blocks, LANES), lambda i: (0, 0)),
        ],
        out_shape=[
            pltpu.VMEM((blocks // 2, block), jnp.bfloat16),
            pltpu.VMEM((blocks // 2, block), jnp.bfloat16),
            jax.ShapeDtypeStruct((blocks, LANES), jnp.float32),
        ],
        scratch_shapes=[
            pltpu.VMEM((blocks, LANES), jnp.float32),
            pltpu.VMEM((blocks, blocks), jnp.bfloat16),
            pltpu.VMEM((blocks, columns), jnp.bfloat16),
            pltpu.VMEM((3, 8, LANES), jnp.float32),
            pltpu.VMEM((2 * levels.shape[0], 8, LANES), jnp.float32),
        ],
        compiler_params=pltpu.CompilerParams(vmem_limit_bytes=32 * MIB),
        name="encode",
    )(levels, rotated, dither, peaks, layout)


def decode_tables(levels_ref):
    count = levels_ref.shape[0]
    lane = lax.broadcasted_iota(jnp.int32, (8, LANES), 1)
    slope = jnp.zeros((8, LANES), jnp.float32)
    intercept = jnp.full((8, LANES), levels_ref[count - 1], jnp.float32)
    for number in range(count - 1):
        low = jnp.full((8, LANES), levels_ref[number], jnp.float32)
        spacing = jnp.full((8, LANES), levels_ref[number + 1], jnp.float32) - low
        slope = jnp.where(lane == number, spacing, slope)
        intercept = jnp.where(lane == number, low - number * spacing, intercept)
    return slope, intercept


def decode_kernel(levels_ref, symbols_ref, *refs):
    out_ref = refs[-1]
    count = levels_ref.shape[0]
    rows, block = out_ref.shape
    wide, deep = 1024, 64
    slope, intercept = decode_tables(levels_ref)
    spacings = [levels_ref[level + 1] - levels_ref[level] for level in range(count - 1)]
    weights = [spacings[0]] + [spacings[level] - spacings[level - 1] for level in range(1, count - 1)] + [-spacings[-1]]

    def some(number, carry):
        down = pl.multiple_of(number // (block // wide) * deep, deep)
        start = number % (block // wide) * wide
        places, tiles = [], []
        for part in range(wide // LANES):
            for row in range(0, deep, 16):
                place = (
                    pl.ds(pl.multiple_of(down + row, 16), 16),
                    pl.ds(pl.multiple_of(start + part * LANES, LANES), LANES),
                )
                symbols = symbols_ref[place].astype(jnp.float32)
                places.append(place)
                tiles += [symbols[:8], symbols[8:]]
        by_table = [at % TABLE_EVERY == 1 for at in range(len(tiles))]
        bounded = {
            at: jnp.minimum(jnp.maximum(tile, 0.0), count - 1.0) for at, tile in enumerate(tiles) if by_table[at]
        }
        index = {at: tile.astype(jnp.int32) for at, tile in bounded.items()}
        lines = {at: (looked_up(slope, which), looked_up(intercept, which)) for at, which in index.items()}
        values = []
        for at, tile in enumerate(tiles):
            if by_table[at]:
                value = bounded[at] * lines[at][0] + lines[at][1]
            else:
                value = jnp.full((8, LANES), levels_ref[count - 1], jnp.float32)
                for level in range(count):
                    value = value + weights[level] * jnp.maximum(tile, float(level))
            values.append(value)
        for at, place in enumerate(places):
            value = jnp.concatenate(values[2 * at : 2 * at + 2], axis=0)
            for ref in refs[:-1]:
                value = value + ref[place]
            out_ref[place] = value
        return carry

    lax.fori_loop(0, rows // deep * (block // wide), some, 0)


def decode(levels, symbols, *others):
    here = pl.BlockSpec(memory_space=pltpu.VMEM)
    return pl.pallas_call(
        decode_kernel,
        in_specs=[pl.BlockSpec(memory_space=pltpu.SMEM), here] + [here] * len(others),
        out_specs=here,
        out_shape=pltpu.VMEM(symbols.shape, jnp.float32),
        compiler_params=pltpu.CompilerParams(vmem_limit_bytes=VMEM_BYTES),
        cost_estimate=pl.CostEstimate(flops=48 * symbols.size, bytes_accessed=6 * symbols.size, transcendentals=0),
        name="decode",
    )(levels, symbols, *others)


def owner_kernel(
    place_ref, total_ref, scales_ref, bits_ref, master_ref, moment_ref, second_ref,
    new_master_ref, new_moment_ref, new_second_ref, copies_ref, table_ref,
):
    rows, block = total_ref.shape
    table = (hadamard(WIDE) * (1.0 / 64.0)).astype(jnp.bfloat16)
    for piece in range(3):
        table_ref[pl.ds(piece * WIDE, WIDE), :] = table
    flips = (1 - 2 * bits_ref[...]).astype(jnp.float32)
    scales = jnp.concatenate([scales_ref[...]] * (WIDE // LANES), axis=1)
    parts = butterflies(total_ref[:, at : at + WIDE] * scales for at in range(0, block, WIDE))
    turned = times_table(jnp.concatenate(parts, axis=0), table_ref[...])
    for number in range(block // WIDE):
        over = slice(number * WIDE, (number + 1) * WIDE)
        grads = turned[number * rows : (number + 1) * rows] * flips[:, over]
        moment = first_decay * moment_ref[:, over] + (1.0 - first_decay) * grads
        second = second_decay * second_ref[:, over] + (1.0 - second_decay) * grads * grads
        master = master_ref[:, over]
        updated = master - learning_rate * (moment / (jnp.sqrt(second) + adam_epsilon) + weight_decay * master)
        new_moment_ref[:, over] = moment
        new_second_ref[:, over] = second
        new_master_ref[:, over] = updated
        rounded = updated.astype(jnp.bfloat16)
        for copy in range(copies_ref.shape[0]):
            copies_ref[copy, :, over] = rounded


def owner(place, total, scales, bits, master, moment, second, copies):
    rows, block = total.shape
    whole = pl.BlockSpec((rows, block), lambda i, place: (0, 0))
    return pl.pallas_call(
        owner_kernel,
        grid_spec=pltpu.PrefetchScalarGridSpec(
            num_scalar_prefetch=1,
            grid=(1,),
            in_specs=[
                whole,
                pl.BlockSpec((rows, LANES), lambda i, place: (place[0], 0)),
                pl.BlockSpec((1, block), lambda i, place: (0, 0)),
                whole,
                whole,
                whole,
            ],
            out_specs=[whole, whole, whole, pl.BlockSpec((copies, rows, block), lambda i, place: (0, 0, 0))],
            scratch_shapes=[pltpu.VMEM((3 * WIDE, WIDE), jnp.bfloat16)],
        ),
        out_shape=[jax.ShapeDtypeStruct((rows, block), jnp.float32)] * 3
        + [jax.ShapeDtypeStruct((copies, rows, block), jnp.bfloat16)],
        compiler_params=pltpu.CompilerParams(vmem_limit_bytes=VMEM_BYTES),
        name="owner",
    )(place, total, scales, bits, master, moment, second)


def reorder_kernel(mine_ref, others_ref, my_slots_ref, other_slots_ref, out_ref, order_ref):
    blocks = out_ref.shape[0]
    half = mine_ref.shape[0]

    @pl.when(pl.program_id(0) == 0)
    def _():
        row = lax.broadcasted_iota(jnp.int32, (blocks, half), 0)
        my_order = (row == my_slots_ref[...]).astype(jnp.float32).astype(jnp.bfloat16)
        other_order = (row == other_slots_ref[...]).astype(jnp.float32).astype(jnp.bfloat16)
        order_ref[...] = jnp.concatenate([my_order, other_order], axis=1)

    here = pl.ds(pl.multiple_of(pl.program_id(0) * out_ref.shape[1], LANES), out_ref.shape[1])
    held = jnp.concatenate([mine_ref[:, here], others_ref[:, here]], axis=0)
    out_ref[...] = jnp.dot(order_ref[...], held, preferred_element_type=jnp.float32).astype(jnp.bfloat16)


def reorder(mine, others, my_slots, other_slots):
    half, block = mine.shape
    columns = 2048
    return pl.pallas_call(
        reorder_kernel,
        grid=(block // columns,),
        in_specs=[
            pl.BlockSpec(memory_space=pltpu.VMEM),
            pl.BlockSpec(memory_space=pltpu.VMEM),
            pl.BlockSpec((1, half), lambda i: (0, 0)),
            pl.BlockSpec((1, half), lambda i: (0, 0)),
        ],
        out_specs=pl.BlockSpec((2 * half, columns), lambda i: (0, i)),
        out_shape=jax.ShapeDtypeStruct((2 * half, block), jnp.bfloat16),
        scratch_shapes=[pltpu.VMEM((2 * half, 2 * half), jnp.bfloat16)],
        compiler_params=pltpu.CompilerParams(vmem_limit_bytes=VMEM_BYTES),
        name="reorder",
    )(mine, others, my_slots, other_slots)


def local(axes, gradient, dither, sign_bits, levels, layout, master, first_moment, second_moment):
    groups = lax.axis_size(axes)
    chips, core = axes[:-1], axes[-1]
    blocks, block = gradient.shape[2:]
    owned = blocks // groups
    bits = sign_bits.reshape(1, block)
    rotated, peaks = rotate(gradient[0, 0], pltpu.with_memory_space_constraint(bits, pltpu.HBM), groups)
    dither, rotated, peaks = lax.optimization_barrier((dither, rotated, peaks))
    peaks = lax.all_to_all(peaks, axes, 0, 0, tiled=True)
    mine, others, scales = encode(core, rotated, dither[0, 0], peaks, layout.reshape(1, blocks), levels)
    theirs = lax.ppermute(others, core, OTHER_CORE)
    merged = decode(levels, theirs, decode(levels, mine))
    pairs = merged.astype(jnp.float16).reshape(groups // 2, owned, block)
    pairs = lax.all_to_all(pairs, chips, 0, 0, tiled=True)
    total = jnp.sum(pairs.astype(jnp.float32), axis=0)
    place = lax.axis_index(axes).reshape(1)
    new_master, new_moment, new_second, copies = owner(
        place, total, scales, bits, master[0], first_moment[0], second_moment[0], groups // 2
    )
    mine = lax.all_to_all(copies, chips, 0, 0, tiled=True)
    others = lax.ppermute(mine, core, OTHER_CORE)
    by_core = layout.reshape(groups // 2, 2, owned)
    which = lax.axis_index(core)
    my_slots = lax.dynamic_index_in_dim(by_core, which, 1, False).reshape(1, blocks // 2)
    other_slots = lax.dynamic_index_in_dim(by_core, 1 - which, 1, False).reshape(1, blocks // 2)
    parameters = reorder(
        mine.reshape(blocks // 2, block), others.reshape(blocks // 2, block), my_slots, other_slots
    )
    return (new_master[None], new_moment[None], new_second[None], parameters[None])


def solution(mesh):
    section, dp = mesh.axis_names
    axes = ("dp_chip", "dp_core")
    split = Mesh(mesh.devices.reshape(mesh.shape[section], mesh.shape[dp] // 2, 2), (section, *axes))
    placed = (
        P(section, axes, None, None),
        P(section, axes, None, None),
        P(),
        P(),
        P(),
        P(section, axes, None),
        P(section, axes, None),
        P(section, axes, None),
    )
    return jax.shard_map(
        functools.partial(local, axes),
        mesh=split,
        in_specs=placed,
        out_specs=(P(section, axes, None), P(section, axes, None), P(section, axes, None), P(section, None, None)),
        check_vma=False,
    )
```

```python
import functools

import jax
import jax.numpy as jnp
from jax import lax
from jax.experimental import pallas as pl
from jax.experimental.pallas import tpu as pltpu
from jax.sharding import Mesh, PartitionSpec as P

adam_epsilon = 1e-08
learning_rate = 0.02
weight_decay = 0.1
first_decay = 0.9
second_decay = 0.95
dither_steps = 256.0

LANES = 128
WIDE = 256
CELLS = 64
CELL_RATE = 31.95
MIB = 1024 * 1024
TABLE_EVERY = 2
VMEM_BYTES = 16 * MIB
OTHER_CORE = ((0, 1), (1, 0))


def hadamard(edge):
    common = lax.broadcasted_iota(jnp.int32, (edge, edge), 0) & lax.broadcasted_iota(jnp.int32, (edge, edge), 1)
    parity = jnp.zeros((edge, edge), jnp.int32)
    for bit in range(edge.bit_length() - 1):
        parity = parity ^ ((common >> bit) & 1)
    return (1 - 2 * parity).astype(jnp.float32)


def three_pieces(values):
    high = values.astype(jnp.bfloat16)
    rest = values - high.astype(jnp.float32)
    middle = rest.astype(jnp.bfloat16)
    low = (rest - middle.astype(jnp.float32)).astype(jnp.bfloat16)
    return high, middle, low


def butterflies(parts):
    parts = list(parts)
    stride = 1
    while stride < len(parts):
        for first in range(len(parts)):
            if not first & stride:
                one, two = parts[first], parts[first + stride]
                parts[first], parts[first + stride] = one + two, one - two
        stride *= 2
    return parts


def times_table(values, table):
    pieces = jnp.concatenate(three_pieces(values), axis=1)
    return jnp.dot(pieces, table, preferred_element_type=jnp.float32)


BY_LANE = lax.GatherDimensionNumbers(
    offset_dims=(),
    collapsed_slice_dims=(1,),
    start_index_map=(1,),
    operand_batching_dims=(0,),
    start_indices_batching_dims=(0,),
)


def looked_up(table, index):
    return lax.gather(table, index[..., None], BY_LANE, (1, 1), mode=lax.GatherScatterMode.PROMISE_IN_BOUNDS)


def rotate_kernel(gradient_ref, bits_ref, rotated_ref, peaks_ref, table_ref, rows_ref):
    step = pl.program_id(0)
    rows, block = gradient_ref.shape

    @pl.when(step == 0)
    def _():
        table = (hadamard(WIDE) * (1.0 / 64.0)).astype(jnp.bfloat16)
        for piece in range(3):
            table_ref[pl.ds(piece * WIDE, WIDE), :] = table

    flips = (1 - 2 * bits_ref[...]).astype(jnp.float32)
    parts = butterflies(gradient_ref[:, at : at + WIDE] * flips[:, at : at + WIDE] for at in range(0, block, WIDE))
    turned = times_table(jnp.concatenate(parts, axis=0), table_ref[...])
    most = jnp.zeros((rows, WIDE), jnp.float32)
    for number in range(block // WIDE):
        part = turned[number * rows : (number + 1) * rows]
        rotated_ref[:, number * WIDE : (number + 1) * WIDE] = part
        most = jnp.maximum(most, jnp.abs(part))
    rows_ref[pl.ds(pl.multiple_of(step * rows, rows), rows), :] = jnp.maximum(most[:, :LANES], most[:, LANES:])

    @pl.when(step == pl.num_programs(0) - 1)
    def _():
        blocks = rows_ref.shape[0]
        lines = [
            jnp.max(jnp.transpose(rows_ref[at : at + LANES, :]), axis=0, keepdims=True) for at in range(0, blocks, LANES)
        ]
        lines = jnp.concatenate(lines, axis=0)
        peaks_ref[...] = jnp.broadcast_to(lines[None], peaks_ref.shape)


def rotate(gradient, bits, groups):
    blocks, block = gradient.shape
    rows = 128
    return pl.pallas_call(
        rotate_kernel,
        grid=(blocks // rows,),
        in_specs=[
            pl.BlockSpec((rows, block), lambda i: (i, 0)),
            pl.BlockSpec((1, block), lambda i: (0, 0)),
        ],
        out_specs=[
            pl.BlockSpec((rows, block), lambda i: (i, 0)),
            pl.BlockSpec((groups, blocks // LANES, LANES), lambda i: (0, 0, 0)),
        ],
        out_shape=[
            jax.ShapeDtypeStruct((blocks, block), jnp.float32),
            jax.ShapeDtypeStruct((groups, blocks // LANES, LANES), jnp.float32),
        ],
        scratch_shapes=[pltpu.VMEM((3 * WIDE, WIDE), jnp.bfloat16), pltpu.VMEM((blocks, LANES), jnp.float32)],
        compiler_params=pltpu.CompilerParams(vmem_limit_bytes=49 * MIB),
        name="rotate",
    )(gradient, bits)


def encode_tables(levels_ref):
    count = levels_ref.shape[0]
    lane = lax.broadcasted_iota(jnp.int32, (8, LANES), 1)
    cell = lane & (CELLS - 1)
    threshold = jnp.full((8, LANES), 4.0, jnp.float32)
    position = jnp.zeros((8, LANES), jnp.int32)
    for number in range(1, count - 1):
        level = jnp.full((8, LANES), levels_ref[number], jnp.float32)
        its_cell = (level * CELL_RATE + 32.0).astype(jnp.int32)
        threshold = jnp.where(its_cell == cell, level, threshold)
        before = (its_cell < cell) | ((its_cell == cell) & (lane >= CELLS))
        position = position + before.astype(jnp.int32)
    slope = jnp.zeros((8, LANES), jnp.float32)
    intercept = jnp.zeros((8, LANES), jnp.float32)
    for number in range(count - 1):
        low = jnp.full((8, LANES), levels_ref[number], jnp.float32)
        high = jnp.full((8, LANES), levels_ref[number + 1], jnp.float32)
        its_slope = 1.0 / (high - low)
        its_intercept = (number + (0.5 / dither_steps - 0.5)) - low * its_slope
        slope = jnp.where(position == number, its_slope, slope)
        intercept = jnp.where(position == number, its_intercept, intercept)
    return threshold, slope, intercept


def line_tables(levels_ref):
    lines = []
    for number in range(levels_ref.shape[0] - 1):
        low = jnp.full((8, LANES), levels_ref[number], jnp.float32)
        slope = 1.0 / (jnp.full((8, LANES), levels_ref[number + 1], jnp.float32) - low)
        lines.append((slope, (number + (0.5 / dither_steps - 0.5)) - low * slope))
    return lines


def encode_kernel(
    core, levels_ref, rotated_ref, dither_ref, peaks_ref, layout_ref, mine_ref, others_ref, scales_ref,
    inverse_ref, order_ref, held_ref, tables_ref, lines_ref,
):
    step = pl.program_id(0)
    blocks = rotated_ref.shape[0]
    columns = held_ref.shape[1]
    count = levels_ref.shape[0]

    @pl.when(step == 0)
    def _():
        lines = jnp.max(peaks_ref[...], axis=0) + 1e-06
        wide = jnp.concatenate([lines[i : i + 1, :] for i in range(blocks // LANES)], axis=1)
        order = lax.broadcasted_iota(jnp.int32, (blocks, blocks), 0) == layout_ref[...]
        order = jnp.transpose(order.astype(jnp.float32))
        by_core = order.reshape(blocks // 16, 2, 8, blocks)
        first, second = by_core[:, 0].reshape(blocks // 2, blocks), by_core[:, 1].reshape(blocks // 2, blocks)
        is_first = lax.axis_index(core) == 0
        grouped = [jnp.where(is_first, first, second), jnp.where(is_first, second, first)]
        order_ref[...] = jnp.concatenate(grouped, axis=0).astype(jnp.bfloat16)
        slot = jnp.sum(jnp.where(order > 0.5, wide, 0.0), axis=1, keepdims=True)
        scales_ref[...] = jnp.broadcast_to(slot, (blocks, LANES))
        for at in range(blocks // LANES):
            square = jnp.broadcast_to(lines[at : at + 1, :], (LANES, LANES))
            inverse_ref[at * LANES : (at + 1) * LANES, :] = 1.0 / jnp.transpose(square)
        for number, table in enumerate(encode_tables(levels_ref)):
            tables_ref[number] = table
        for number, (slope, intercept) in enumerate(line_tables(levels_ref)):
            lines_ref[2 * number] = slope
            lines_ref[2 * number + 1] = intercept

    threshold, slope, intercept = tables_ref[0], tables_ref[1], tables_ref[2]
    deep = 128

    def some_rows(number, carry):
        start = pl.multiple_of(number * deep, deep)
        tiles = [(row, part) for part in range(columns // LANES) for row in range(0, deep, 8)]

        def over(row, part, height=8):
            return pl.ds(pl.multiple_of(start + row, height), height), slice(part * LANES, (part + 1) * LANES)

        def whole(row, part):
            return pl.ds(pl.multiple_of(start + row, 8), 8), pl.ds(pl.multiple_of(step * columns + part * LANES, LANES), LANES)

        ratios = {tile: rotated_ref[whole(*tile)] * inverse_ref[over(tile[0], 0)] for tile in tiles}
        by_table = tiles[1::2]
        cells = {tile: (ratios[tile] * CELL_RATE + 32.0).astype(jnp.int32) for tile in by_table}
        limits = {tile: looked_up(threshold, cells[tile]) for tile in by_table}
        sides = {
            tile: jnp.where(ratios[tile] >= limits[tile], cells[tile] + CELLS, cells[tile]) for tile in by_table
        }
        slopes = {tile: looked_up(slope, sides[tile]) for tile in by_table}
        intercepts = {tile: looked_up(intercept, sides[tile]) for tile in by_table}
        values = {}
        for tile in tiles:
            ratio = ratios[tile]
            if tile in slopes:
                value = ratio * slopes[tile] + intercepts[tile]
            else:
                its_slope, its_intercept = lines_ref[0], lines_ref[1]
                for level in range(1, count - 1):
                    above = ratio >= levels_ref[level]
                    its_slope = jnp.where(above, lines_ref[2 * level], its_slope)
                    its_intercept = jnp.where(above, lines_ref[2 * level + 1], its_intercept)
                value = ratio * its_slope + its_intercept
            values[tile] = value + dither_ref[whole(*tile)].astype(jnp.float32) * (1.0 / dither_steps)
        for part in range(columns // LANES):
            for row in range(0, deep, 16):
                pair = jnp.concatenate([values[row, part], values[row + 8, part]], axis=0)
                held_ref[over(row, part, 16)] = pair.astype(jnp.bfloat16)
        return carry

    lax.fori_loop(0, blocks // deep, some_rows, 0)
    slotted = jnp.dot(order_ref[...], held_ref[...], preferred_element_type=jnp.float32)

    there = pl.ds(pl.multiple_of(step * columns, columns), columns)
    mine_ref[:, there] = slotted[: blocks // 2].astype(jnp.bfloat16)
    others_ref[:, there] = slotted[blocks // 2 :].astype(jnp.bfloat16)


def encode(core, rotated, dither, peaks, layout, levels):
    blocks, block = rotated.shape
    columns = 2048
    return pl.pallas_call(
        functools.partial(encode_kernel, core),
        grid=(block // columns,),
        in_specs=[
            pl.BlockSpec(memory_space=pltpu.SMEM),
            pl.BlockSpec(memory_space=pltpu.VMEM),
            pl.BlockSpec(memory_space=pltpu.VMEM),
            pl.BlockSpec(peaks.shape, lambda i: (0, 0, 0)),
            pl.BlockSpec((1, blocks), lambda i: (0, 0)),
        ],
        out_specs=[
            pl.BlockSpec(memory_space=pltpu.VMEM),
            pl.BlockSpec(memory_space=pltpu.VMEM),
            pl.BlockSpec((blocks, LANES), lambda i: (0, 0)),
        ],
        out_shape=[
            pltpu.VMEM((blocks // 2, block), jnp.bfloat16),
            pltpu.VMEM((blocks // 2, block), jnp.bfloat16),
            jax.ShapeDtypeStruct((blocks, LANES), jnp.float32),
        ],
        scratch_shapes=[
            pltpu.VMEM((blocks, LANES), jnp.float32),
            pltpu.VMEM((blocks, blocks), jnp.bfloat16),
            pltpu.VMEM((blocks, columns), jnp.bfloat16),
            pltpu.VMEM((3, 8, LANES), jnp.float32),
            pltpu.VMEM((2 * levels.shape[0], 8, LANES), jnp.float32),
        ],
        compiler_params=pltpu.CompilerParams(vmem_limit_bytes=32 * MIB),
        name="encode",
    )(levels, rotated, dither, peaks, layout)


def decode_tables(levels_ref):
    count = levels_ref.shape[0]
    lane = lax.broadcasted_iota(jnp.int32, (8, LANES), 1)
    slope = jnp.zeros((8, LANES), jnp.float32)
    intercept = jnp.full((8, LANES), levels_ref[count - 1], jnp.float32)
    for number in range(count - 1):
        low = jnp.full((8, LANES), levels_ref[number], jnp.float32)
        spacing = jnp.full((8, LANES), levels_ref[number + 1], jnp.float32) - low
        slope = jnp.where(lane == number, spacing, slope)
        intercept = jnp.where(lane == number, low - number * spacing, intercept)
    return slope, intercept


def decode_kernel(levels_ref, symbols_ref, *refs):
    out_ref = refs[-1]
    count = levels_ref.shape[0]
    rows, block = out_ref.shape
    wide, deep = 1024, 128
    slope, intercept = decode_tables(levels_ref)
    spacings = [levels_ref[level + 1] - levels_ref[level] for level in range(count - 1)]
    weights = [spacings[0]] + [spacings[level] - spacings[level - 1] for level in range(1, count - 1)] + [-spacings[-1]]

    def some(number, carry):
        down = pl.multiple_of(number // (block // wide) * deep, deep)
        start = number % (block // wide) * wide
        places, tiles = [], []
        for part in range(wide // LANES):
            for row in range(0, deep, 16):
                place = (
                    pl.ds(pl.multiple_of(down + row, 16), 16),
                    pl.ds(pl.multiple_of(start + part * LANES, LANES), LANES),
                )
                symbols = symbols_ref[place].astype(jnp.float32)
                places.append(place)
                tiles += [symbols[:8], symbols[8:]]
        by_table = [at % TABLE_EVERY == 1 for at in range(len(tiles))]
        bounded = {
            at: jnp.minimum(jnp.maximum(tile, 0.0), count - 1.0) for at, tile in enumerate(tiles) if by_table[at]
        }
        index = {at: tile.astype(jnp.int32) for at, tile in bounded.items()}
        lines = {at: (looked_up(slope, which), looked_up(intercept, which)) for at, which in index.items()}
        values = []
        for at, tile in enumerate(tiles):
            if by_table[at]:
                value = bounded[at] * lines[at][0] + lines[at][1]
            else:
                value = jnp.full((8, LANES), levels_ref[count - 1], jnp.float32)
                for level in range(count):
                    value = value + weights[level] * jnp.maximum(tile, float(level))
            values.append(value)
        for at, place in enumerate(places):
            value = jnp.concatenate(values[2 * at : 2 * at + 2], axis=0)
            for ref in refs[:-1]:
                value = value + ref[place]
            out_ref[place] = value
        return carry

    lax.fori_loop(0, rows // deep * (block // wide), some, 0)


def decode(levels, symbols, *others):
    here = pl.BlockSpec(memory_space=pltpu.VMEM)
    return pl.pallas_call(
        decode_kernel,
        in_specs=[pl.BlockSpec(memory_space=pltpu.SMEM), here] + [here] * len(others),
        out_specs=here,
        out_shape=pltpu.VMEM(symbols.shape, jnp.float32),
        compiler_params=pltpu.CompilerParams(vmem_limit_bytes=VMEM_BYTES),
        cost_estimate=pl.CostEstimate(flops=48 * symbols.size, bytes_accessed=6 * symbols.size, transcendentals=0),
        name="decode",
    )(levels, symbols, *others)


def owner_kernel(
    place_ref, total_ref, scales_ref, bits_ref, master_ref, moment_ref, second_ref,
    new_master_ref, new_moment_ref, new_second_ref, copies_ref, table_ref,
):
    rows, block = total_ref.shape
    table = (hadamard(WIDE) * (1.0 / 64.0)).astype(jnp.bfloat16)
    for piece in range(3):
        table_ref[pl.ds(piece * WIDE, WIDE), :] = table
    flips = (1 - 2 * bits_ref[...]).astype(jnp.float32)
    scales = jnp.concatenate([scales_ref[...]] * (WIDE // LANES), axis=1)
    parts = butterflies(total_ref[:, at : at + WIDE] * scales for at in range(0, block, WIDE))
    turned = times_table(jnp.concatenate(parts, axis=0), table_ref[...])
    for number in range(block // WIDE):
        over = slice(number * WIDE, (number + 1) * WIDE)
        grads = turned[number * rows : (number + 1) * rows] * flips[:, over]
        moment = first_decay * moment_ref[:, over] + (1.0 - first_decay) * grads
        second = second_decay * second_ref[:, over] + (1.0 - second_decay) * grads * grads
        master = master_ref[:, over]
        updated = master - learning_rate * (moment / (jnp.sqrt(second) + adam_epsilon) + weight_decay * master)
        new_moment_ref[:, over] = moment
        new_second_ref[:, over] = second
        new_master_ref[:, over] = updated
        rounded = updated.astype(jnp.bfloat16)
        for copy in range(copies_ref.shape[0]):
            copies_ref[copy, :, over] = rounded


def owner(place, total, scales, bits, master, moment, second, copies):
    rows, block = total.shape
    whole = pl.BlockSpec((rows, block), lambda i, place: (0, 0))
    return pl.pallas_call(
        owner_kernel,
        grid_spec=pltpu.PrefetchScalarGridSpec(
            num_scalar_prefetch=1,
            grid=(1,),
            in_specs=[
                whole,
                pl.BlockSpec((rows, LANES), lambda i, place: (place[0], 0)),
                pl.BlockSpec((1, block), lambda i, place: (0, 0)),
                whole,
                whole,
                whole,
            ],
            out_specs=[whole, whole, whole, pl.BlockSpec((copies, rows, block), lambda i, place: (0, 0, 0))],
            scratch_shapes=[pltpu.VMEM((3 * WIDE, WIDE), jnp.bfloat16)],
        ),
        out_shape=[jax.ShapeDtypeStruct((rows, block), jnp.float32)] * 3
        + [jax.ShapeDtypeStruct((copies, rows, block), jnp.bfloat16)],
        compiler_params=pltpu.CompilerParams(vmem_limit_bytes=VMEM_BYTES),
        name="owner",
    )(place, total, scales, bits, master, moment, second)


def reorder_kernel(mine_ref, others_ref, my_slots_ref, other_slots_ref, out_ref, order_ref):
    blocks = out_ref.shape[0]
    half = mine_ref.shape[0]

    @pl.when(pl.program_id(0) == 0)
    def _():
        row = lax.broadcasted_iota(jnp.int32, (blocks, half), 0)
        my_order = (row == my_slots_ref[...]).astype(jnp.float32).astype(jnp.bfloat16)
        other_order = (row == other_slots_ref[...]).astype(jnp.float32).astype(jnp.bfloat16)
        order_ref[...] = jnp.concatenate([my_order, other_order], axis=1)

    here = pl.ds(pl.multiple_of(pl.program_id(0) * out_ref.shape[1], LANES), out_ref.shape[1])
    held = jnp.concatenate([mine_ref[:, here], others_ref[:, here]], axis=0)
    out_ref[...] = jnp.dot(order_ref[...], held, preferred_element_type=jnp.float32).astype(jnp.bfloat16)


def reorder(mine, others, my_slots, other_slots):
    half, block = mine.shape
    columns = 2048
    return pl.pallas_call(
        reorder_kernel,
        grid=(block // columns,),
        in_specs=[
            pl.BlockSpec(memory_space=pltpu.VMEM),
            pl.BlockSpec(memory_space=pltpu.VMEM),
            pl.BlockSpec((1, half), lambda i: (0, 0)),
            pl.BlockSpec((1, half), lambda i: (0, 0)),
        ],
        out_specs=pl.BlockSpec((2 * half, columns), lambda i: (0, i)),
        out_shape=jax.ShapeDtypeStruct((2 * half, block), jnp.bfloat16),
        scratch_shapes=[pltpu.VMEM((2 * half, 2 * half), jnp.bfloat16)],
        compiler_params=pltpu.CompilerParams(vmem_limit_bytes=VMEM_BYTES),
        name="reorder",
    )(mine, others, my_slots, other_slots)


def local(axes, gradient, dither, sign_bits, levels, layout, master, first_moment, second_moment):
    groups = lax.axis_size(axes)
    chips, core = axes[:-1], axes[-1]
    blocks, block = gradient.shape[2:]
    owned = blocks // groups
    bits = sign_bits.reshape(1, block)
    rotated, peaks = rotate(gradient[0, 0], pltpu.with_memory_space_constraint(bits, pltpu.HBM), groups)
    dither, rotated, peaks = lax.optimization_barrier((dither, rotated, peaks))
    peaks = lax.all_to_all(peaks, axes, 0, 0, tiled=True)
    mine, others, scales = encode(core, rotated, dither[0, 0], peaks, layout.reshape(1, blocks), levels)
    theirs = lax.ppermute(others, core, OTHER_CORE)
    merged = decode(levels, theirs, decode(levels, mine))
    pairs = merged.astype(jnp.float16).reshape(groups // 2, owned, block)
    pairs = lax.all_to_all(pairs, chips, 0, 0, tiled=True)
    total = jnp.sum(pairs.astype(jnp.float32), axis=0)
    place = lax.axis_index(axes).reshape(1)
    new_master, new_moment, new_second, copies = owner(
        place, total, scales, bits, master[0], first_moment[0], second_moment[0], groups // 2
    )
    mine = lax.all_to_all(copies, chips, 0, 0, tiled=True)
    others = lax.ppermute(mine, core, OTHER_CORE)
    by_core = layout.reshape(groups // 2, 2, owned)
    which = lax.axis_index(core)
    my_slots = lax.dynamic_index_in_dim(by_core, which, 1, False).reshape(1, blocks // 2)
    other_slots = lax.dynamic_index_in_dim(by_core, 1 - which, 1, False).reshape(1, blocks // 2)
    parameters = reorder(
        mine.reshape(blocks // 2, block), others.reshape(blocks // 2, block), my_slots, other_slots
    )
    return (new_master[None], new_moment[None], new_second[None], parameters[None])


def solution(mesh):
    section, dp = mesh.axis_names
    axes = ("dp_chip", "dp_core")
    split = Mesh(mesh.devices.reshape(mesh.shape[section], mesh.shape[dp] // 2, 2), (section, *axes))
    placed = (
        P(section, axes, None, None),
        P(section, axes, None, None),
        P(),
        P(),
        P(),
        P(section, axes, None),
        P(section, axes, None),
        P(section, axes, None),
    )
    return jax.shard_map(
        functools.partial(local, axes),
        mesh=split,
        in_specs=placed,
        out_specs=(P(section, axes, None), P(section, axes, None), P(section, axes, None), P(section, None, None)),
        check_vma=False,
    )
```
